256 devices in a mesh: ctx: 32 (over x, z), head: 8 (over y, core).
Axes of the slice: x: 4, y: 4, z: 8, core: 2. Of those that a mesh axis runs over, the one named last changes fastest.
Arguments:
- queries: bfloat16 [32768, 4096], P('ctx', 'head'), may hold values from -60 to 60
- keys: bfloat16 [32768, 4096], P('ctx', 'head'), may hold values from -6 to 6
- values: bfloat16 [32768, 4096], P('ctx', 'head'), may hold values from -6 to 6
- gain: float32 [4096], P('head'), may hold values from 0.25 to 1.75
- grad_normed: bfloat16 [32768, 4096], P('ctx', 'head'), may hold values from -6 to 6
Outputs:
- normed: bfloat16 [32768, 4096], P('ctx', 'head')
- grad_queries: bfloat16 [32768, 4096], P('ctx', 'head')
- grad_keys: bfloat16 [32768, 4096], P('ctx', 'head')
- grad_values: bfloat16 [32768, 4096], P('ctx', 'head')
The draws below stay inside these ranges and needn't reach their ends.
All inputs are finite; a program needn't handle non-finite values.
Results may differ from the reference program's by a relative error of at most 0.0057.
Values sent between devices are 32-bit elements; how exact they have to be, the bound alone decides.
No kernel may reach another device: no remote copies, remote signals or barrier semaphores. Data moves between devices by JAX's collectives and lax.ppermute only.
A program may use at most 128 MiB of HBM per device.

```python
import jax
import jax.numpy as jnp
from jax import lax

HEAD_DIM = 128
GROUP = 512
HEADS = 32
WIDTH = 4096
TOKENS = 32768


def draw_queries(key, part):
    column = jnp.arange(HEADS * HEAD_DIM) // HEAD_DIM
    ratio = 10.0
    base = jnp.clip(jax.random.normal(key, (TOKENS, HEADS * HEAD_DIM), jnp.float32), -6.0, 6.0)
    spread = jnp.exp(jnp.log(ratio) * column.astype(jnp.float32) / max(HEADS - 1, 1))
    return (base * spread[None, :]).astype(jnp.bfloat16)


def levels(stream_key, shape, shards, low, high):
    level = 1.0
    for dim, blocks in shards:
        heights = jax.random.uniform(jax.random.fold_in(jax.random.fold_in(stream_key, 6), dim), (blocks,), jnp.float32, low / len(shards), high / len(shards))
        level = level * jnp.repeat(jnp.exp(heights), shape[dim] // blocks).reshape((-1,) + (1,) * (len(shape) - 1 - dim))
    return level


def scatter_about(stream_key, shape, scale, reach, cuts=(), held_as=jnp.bfloat16):
    factor_of = levels(stream_key, shape, cuts, -0.22, 0.18) if cuts else 1.0
    values = jax.random.normal(stream_key, shape, jnp.float32) * scale * factor_of
    return jnp.minimum(jnp.maximum(values, -reach), reach).astype(held_as)


def setup_inputs(seed: int = 0) -> dict:
    streams_of = jax.random.split(jax.random.key(seed), 6)
    queries = draw_queries(jax.random.fold_in(streams_of[5], 71), 0)
    keys = scatter_about(streams_of[1], (TOKENS, WIDTH), 1.0, 6.0, ((0, 32), (1, 8)))
    values = scatter_about(streams_of[2], (TOKENS, WIDTH), 1.0, 6.0, ((0, 32), (1, 8)))
    gain = jnp.clip(1.0 + 0.15 * jax.random.normal(streams_of[3], (WIDTH,), jnp.float32), 0.25, 1.75)
    grad_normed = scatter_about(streams_of[4], (TOKENS, WIDTH), 1.0, 6.0, ((0, 32), (1, 8)))
    return dict(queries=queries, keys=keys, values=values, gain=gain, grad_normed=grad_normed)


EPSILON = 1e-06

def split_heads(array, blocks):
    return array.reshape(blocks, GROUP, HEADS, HEAD_DIM).transpose(2, 0, 1, 3)

def merge_heads(array, tokens):
    return array.transpose(1, 2, 0, 3).reshape(tokens, HEADS * HEAD_DIM)

def causal_mask():
    return jnp.arange(GROUP)[:, None] >= jnp.arange(GROUP)[None, :]

def head_states(key_wide, value_wide):
    moments = jnp.einsum('ncd,nce->nde', key_wide, value_wide)
    running = jnp.cumsum(moments, axis=0)
    state = jnp.concatenate([jnp.zeros_like(moments[:1]), running[:-1]], axis=0)
    return state.astype(jnp.bfloat16)

def head_probs(query_wide, key_wide):
    scores = jnp.einsum('ncd,nsd->ncs', query_wide, key_wide)
    return jnp.where(causal_mask()[None], scores, 0.0).astype(jnp.bfloat16)

def head_forward(operands):
    query_head, key_head, value_head = operands
    query_wide = query_head.astype(jnp.float32)
    key_wide = key_head.astype(jnp.float32)
    value_wide = value_head.astype(jnp.float32)
    state_half = head_states(key_wide, value_wide)
    probs_half = head_probs(query_wide, key_wide)
    return jnp.einsum('ncd,nde->nce', query_wide, state_half.astype(jnp.float32)) + jnp.einsum('ncs,nse->nce', probs_half.astype(jnp.float32), value_wide)

def head_backward(operands):
    query_head, key_head, value_head, grad_head = operands
    query_wide = query_head.astype(jnp.float32)
    key_wide = key_head.astype(jnp.float32)
    value_wide = value_head.astype(jnp.float32)
    grad_wide = grad_head.astype(jnp.float32)
    state_wide = head_states(key_wide, value_wide).astype(jnp.float32)
    probs_wide = head_probs(query_wide, key_wide).astype(jnp.float32)
    comoments = jnp.einsum('ncd,nce->nde', query_wide, grad_wide)
    later = jnp.flip(jnp.cumsum(jnp.flip(comoments, 0), axis=0), 0)
    suffix = jnp.concatenate([later[1:], jnp.zeros_like(comoments[:1])], axis=0)
    suffix_wide = suffix.astype(jnp.bfloat16).astype(jnp.float32)
    grad_scores = jnp.einsum('nce,nse->ncs', grad_wide, value_wide)
    grad_scores = jnp.where(causal_mask()[None], grad_scores, 0.0).astype(jnp.bfloat16).astype(jnp.float32)
    grad_query = (jnp.einsum('nce,nde->ncd', grad_wide, state_wide) + jnp.einsum('ncs,nsd->ncd', grad_scores, key_wide)).astype(jnp.bfloat16)
    grad_key = (jnp.einsum('nse,nde->nsd', value_wide, suffix_wide) + jnp.einsum('ncs,ncd->nsd', grad_scores, query_wide)).astype(jnp.bfloat16)
    grad_value = (jnp.einsum('nsd,nde->nse', key_wide, suffix_wide) + jnp.einsum('ncs,nce->nse', probs_wide, grad_wide)).astype(jnp.bfloat16)
    return (grad_query, grad_key, grad_value)

def reference(queries, keys, values, gain, grad_normed):
    tokens = queries.shape[0]
    blocks = tokens // GROUP
    query_split = split_heads(queries, blocks)
    key_split = split_heads(keys, blocks)
    value_split = split_heads(values, blocks)
    attended = lax.map(head_forward, (query_split, key_split, value_split))
    width = HEADS * HEAD_DIM
    squares = lax.optimization_barrier(jnp.sum(attended * attended, axis=(0, 3)))
    rms = jnp.sqrt(squares / width + EPSILON)[None, :, :, None]
    unit = attended / rms
    gain_heads = gain.reshape(HEADS, 1, 1, HEAD_DIM)
    normed = (unit * gain_heads).astype(jnp.bfloat16)
    gated = gain_heads * split_heads(grad_normed, blocks).astype(jnp.float32)
    mean_dot = lax.optimization_barrier(jnp.sum(gated * unit, axis=(0, 3))) / width
    grad_attn = ((gated - unit * mean_dot[None, :, :, None]) / rms).astype(jnp.bfloat16)
    grad_query, grad_key, grad_value = lax.map(head_backward, (query_split, key_split, value_split, grad_attn))
    return (merge_heads(normed, tokens), merge_heads(grad_query, tokens), merge_heads(grad_key, tokens), merge_heads(grad_value, tokens))
```

```python
import jax
import jax.numpy as jnp
from jax import lax
from jax.experimental import pallas as pl
from jax.experimental.pallas import tpu as pltpu
from jax.sharding import PartitionSpec as P

HEAD_DIM = 128
GROUP = 512
HALF = 256
EPSILON = 1e-06
XS, ZS = 4, 8
HEADS_LOCAL = 4
F32 = jnp.float32
BF16 = jnp.bfloat16


NT = (((1,), (1,)), ((), ()))
TN = (((0,), (0,)), ((), ()))
NN = (((1,), (0,)), ((), ()))


def mm(a, b, dims):
    return lax.dot_general(a, b, dims, preferred_element_type=F32)


def mm_exact(a, b, dims):
    return lax.dot_general(a, b, dims, preferred_element_type=F32, precision=lax.Precision.HIGHEST)


def causal(rows, cols, row0, col0, flip):
    t = lax.broadcasted_iota(jnp.int32, (rows, cols), 0) + row0
    s = lax.broadcasted_iota(jnp.int32, (rows, cols), 1) + col0
    return (s >= t) if flip else (t >= s)


def call(kernel, grid, in_specs, out_specs, out_shape, scratch=(), flops=0, nbytes=0, vmem=16 << 20):
    return pl.pallas_call(
        kernel,
        grid=grid,
        in_specs=in_specs,
        out_specs=out_specs,
        out_shape=out_shape,
        scratch_shapes=list(scratch),
        compiler_params=pltpu.CompilerParams(vmem_limit_bytes=vmem),
        cost_estimate=pl.CostEstimate(flops=flops, bytes_accessed=nbytes, transcendentals=0),
    )


def struct(shape, dtype):
    return jax.ShapeDtypeStruct(shape, dtype)


def moment_kernel(k_ref, v_ref, total_ref, first_ref):
    first = mm(k_ref[:GROUP], v_ref[:GROUP], TN)
    second = mm(k_ref[GROUP:], v_ref[GROUP:], TN)
    first_ref[...] = first
    total_ref[...] = first + second


def moments(k, v):
    spec = pl.BlockSpec((2 * GROUP, HEAD_DIM), lambda h: (0, h))
    out = pl.BlockSpec((HEAD_DIM, HEAD_DIM), lambda h: (h, 0))
    return call(
        moment_kernel,
        (HEADS_LOCAL,),
        [spec, spec],
        [out, out],
        [struct((512, 128), F32)] * 2,
        flops=8 * 2 * 512 * 128 * 128,
        nbytes=2 << 20,
    )(k, v)


def local_kernel(q_ref, k_ref, v_ref, out_ref):
    for r in (0, 1):
        n = HALF * (r + 1)
        rows = pl.ds(r * HALF, HALF)
        scores = mm(q_ref[rows], k_ref[:n], NT)
        probs = jnp.where(causal(HALF, n, r * HALF, 0, False), scores, 0.0).astype(BF16)
        out_ref[rows] = mm(probs, v_ref[:n], NN)


def local_attention(q, k, v):
    spec = pl.BlockSpec((GROUP, HEAD_DIM), lambda h, j: (j, h))
    return call(
        local_kernel,
        (HEADS_LOCAL, 2),
        [spec] * 3,
        spec,
        struct((1024, 512), F32),
        flops=8 * 2 * 2 * 512 * 512 * 128,
        nbytes=5 << 20,
    )(q, k, v)


def state_of(incoming_ref, first_ref, h, second):
    rows = pl.ds(h * HEAD_DIM, HEAD_DIM)
    before = jnp.where(second, first_ref[rows], 0.0)
    return (incoming_ref[rows] + before).astype(BF16)


def attend_kernel(q_ref, local_ref, g_ref, gain_ref, incoming_ref, first_ref, att_ref, stats_ref, acc_ref):
    i = pl.program_id(0)
    square = jnp.zeros((HALF, HEAD_DIM), F32)
    inner = jnp.zeros((HALF, HEAD_DIM), F32)
    for h in range(HEADS_LOCAL):
        cols = slice(h * HEAD_DIM, (h + 1) * HEAD_DIM)
        state = state_of(incoming_ref, first_ref, h, i >= 2)
        att = mm(q_ref[:, cols], state, NN) + local_ref[:, cols]
        att_ref[:, cols] = att
        gated = gain_ref[:, cols] * g_ref[:, cols].astype(F32)
        square = square + att * att
        inner = inner + gated * att
    both = jnp.concatenate([square, inner], axis=1)
    row = lax.broadcasted_iota(jnp.int32, (16, 256), 0)
    lane = lax.broadcasted_iota(jnp.int32, (16, 256), 1)

    @pl.when(i == 0)
    def _():
        acc_ref[...] = jnp.zeros_like(acc_ref)

    for c in (0, 1):
        pick = (row == 2 * (2 * i + c) + (lane >= 128).astype(jnp.int32)).astype(F32)
        acc_ref[...] += mm_exact(pick, both[c * 128 : (c + 1) * 128], NT)

    @pl.when(i == 3)
    def _():
        stats_ref[...] = jnp.broadcast_to(acc_ref[...][None], stats_ref.shape)


def attend(q, local, g, gain, incoming, first):
    chunk = pl.BlockSpec((HALF, 512), lambda i: (i, 0))
    whole = pl.BlockSpec((512, 128), lambda i: (0, 0))
    return call(
        attend_kernel,
        (4,),
        [chunk, chunk, chunk, pl.BlockSpec((1, 512), lambda i: (0, 0)), whole, whole],
        [chunk, pl.BlockSpec((8, 16, 128), lambda i: (0, 0, 0))],
        [struct((1024, 512), F32), struct((8, 16, 128), F32)],
        scratch=[pltpu.VMEM((16, 128), F32)],
        flops=2 * 1024 * 512 * 128,
        nbytes=6 << 20,
    )(q, local, g, gain, incoming, first)


def norm_kernel(att_ref, g_ref, q_ref, gain_ref, stats_ref, normed_ref, ga_ref, total_ref, last_ref):
    i = pl.program_id(0)
    sums = jnp.sum(stats_ref[...], axis=0)
    row = lax.broadcasted_iota(jnp.int32, (16, 256), 0)
    lane = lax.broadcasted_iota(jnp.int32, (16, 256), 1)
    wide = []
    for c in (0, 1):
        pick = (row == 2 * (2 * i + c) + (lane >= 128).astype(jnp.int32)).astype(F32)
        wide.append(mm_exact(sums, pick, TN))
    wide = jnp.concatenate(wide, axis=0)
    rms = jnp.sqrt(wide[:, :128] * (1.0 / 4096) + EPSILON)
    inverse = 1.0 / rms
    mean = wide[:, 128:] * inverse * (1.0 / 4096)

    @pl.when(i == 0)
    def _():
        total_ref[...] = jnp.zeros_like(total_ref)
        last_ref[...] = jnp.zeros_like(last_ref)

    for h in range(HEADS_LOCAL):
        cols = slice(h * HEAD_DIM, (h + 1) * HEAD_DIM)
        rows = slice(h * HEAD_DIM, (h + 1) * HEAD_DIM)
        gain = gain_ref[:, cols]
        unit = att_ref[:, cols] * inverse
        normed_ref[:, cols] = (unit * gain).astype(BF16)
        ga = ((gain * g_ref[:, cols].astype(F32) - unit * mean) * inverse).astype(BF16)
        ga_ref[:, cols] = ga
        part = mm(q_ref[:, cols], ga, TN)
        total_ref[rows] += part
        last_ref[rows] += jnp.where(i >= 2, part, 0.0)


def norm(att, g, q, gain, stats):
    chunk = pl.BlockSpec((HALF, 512), lambda i: (i, 0))
    whole = pl.BlockSpec((512, 128), lambda i: (0, 0))
    return call(
        norm_kernel,
        (4,),
        [chunk, chunk, chunk, pl.BlockSpec((1, 512), lambda i: (0, 0)), pl.BlockSpec((8, 16, 128), lambda i: (0, 0, 0))],
        [chunk, chunk, whole, whole],
        [struct((1024, 512), BF16), struct((1024, 512), BF16), struct((512, 128), F32), struct((512, 128), F32)],
        flops=2 * 1024 * 512 * 128,
        nbytes=6 << 20,
    )(att, g, q, gain, stats)


def back_kernel(q_ref, k_ref, v_ref, ga_ref, incoming_ref, first_ref, gq_ref, gk_ref, gv_ref):
    second = pl.program_id(1) == 1
    state = (incoming_ref[...] + jnp.where(second, first_ref[...], 0.0)).astype(BF16)
    for r in (0, 1):
        n = HALF * (r + 1)
        rows = pl.ds(r * HALF, HALF)
        grads = mm(ga_ref[rows], v_ref[:n], NT)
        grads = jnp.where(causal(HALF, n, r * HALF, 0, False), grads, 0.0).astype(BF16)
        gq = mm(ga_ref[rows], state, NT) + mm(grads, k_ref[:n], NN)
        gq_ref[rows] = gq.astype(BF16)
    for c in (0, 1):
        rows = pl.ds(c * HALF, HALF)
        rest = pl.ds(c * HALF, GROUP - c * HALF)
        n = GROUP - c * HALF
        mask = causal(HALF, n, 0, 0, True)
        grads = jnp.where(mask, mm(v_ref[rows], ga_ref[rest], NT), 0.0).astype(BF16)
        gk_ref[rows] = mm(grads, q_ref[rest], NN)
        probs = jnp.where(mask, mm(k_ref[rows], q_ref[rest], NT), 0.0).astype(BF16)
        gv_ref[rows] = mm(probs, ga_ref[rest], NN)


def back(q, k, v, ga, incoming, first):
    spec = pl.BlockSpec((GROUP, HEAD_DIM), lambda h, j: (j, h))
    state = pl.BlockSpec((HEAD_DIM, HEAD_DIM), lambda h, j: (h, 0))
    return call(
        back_kernel,
        (HEADS_LOCAL, 2),
        [spec] * 4 + [state] * 2,
        [spec] * 3,
        [struct((1024, 512), BF16), struct((1024, 512), F32), struct((1024, 512), F32)],
        flops=8 * 6 * 2 * 512 * 512 * 128,
        nbytes=9 << 20,
    )(q, k, v, ga, incoming, first)


def last_kernel(k_ref, v_ref, gk_local_ref, gv_local_ref, arriving_ref, last_ref, gk_ref, gv_ref):
    first = pl.program_id(1) == 0
    suffix = (arriving_ref[...] + jnp.where(first, last_ref[...], 0.0)).astype(BF16)
    gk_ref[...] = (mm(v_ref[...], suffix, NT) + gk_local_ref[...]).astype(BF16)
    gv_ref[...] = (mm(k_ref[...], suffix, NN) + gv_local_ref[...]).astype(BF16)


def finish(k, v, gk_local, gv_local, arriving, last):
    spec = pl.BlockSpec((GROUP, HEAD_DIM), lambda h, j: (j, h))
    state = pl.BlockSpec((HEAD_DIM, HEAD_DIM), lambda h, j: (h, 0))
    return call(
        last_kernel,
        (HEADS_LOCAL, 2),
        [spec] * 4 + [state] * 2,
        [spec] * 2,
        [struct((1024, 512), BF16)] * 2,
        flops=2 * 2 * 1024 * 512 * 128,
        nbytes=8 << 20,
    )(k, v, gk_local, gv_local, arriving, last)


def running_kernel(reverse, pieces_ref, a_ref, b_ref, c_ref, out_ref):
    run = a_ref[...] + b_ref[...] + c_ref[...]
    order = range(ZS - 1, -1, -1) if reverse else range(ZS)
    for z in order:
        out_ref[z] = run
        run = run + pieces_ref[z]


def running(pieces, offsets, reverse):
    def kernel(*refs):
        running_kernel(reverse, *refs)

    shape = (ZS, 512 // ZS, 128)
    whole = pl.BlockSpec(shape, lambda i: (0, 0, 0))
    part = pl.BlockSpec(shape[1:], lambda i: (0, 0))
    return call(kernel, (1,), [whole] + [part] * 3, whole, struct(shape, F32), flops=8 * 8192, nbytes=1 << 19)(
        pieces, *offsets
    )


LINES = [[x * ZS + z for z in range(ZS)] for x in range(XS)]


def exchange(value):
    return lax.all_to_all(value, "ctx", 0, 0, tiled=True, axis_index_groups=LINES)


def prefix(total, reverse):
    pieces = exchange(total.reshape(ZS, 512 // ZS, 128))
    line = jnp.sum(pieces, axis=0)
    offsets = []
    for d in range(1, XS):
        pairs = [(x * ZS + z, (x + d) * ZS + z) for x in range(XS - d) for z in range(ZS)]
        if reverse:
            pairs = [(b, a) for a, b in pairs]
        offsets.append(lax.ppermute(line, "ctx", pairs))
    return exchange(running(pieces, offsets, reverse)).reshape(512, 128)


def on_device(queries, keys, values, gain, grad_normed):
    gain = gain.reshape(1, 512)
    total, first = moments(keys, values)
    incoming = prefix(total, False)
    local = local_attention(queries, keys, values)
    att, stats = attend(queries, local, grad_normed, gain, incoming, first)
    stats = lax.all_to_all(stats, "head", 0, 0, tiled=True)
    normed, ga, cototal, last = norm(att, grad_normed, queries, gain, stats)
    arriving = prefix(cototal, True)
    gq, gk_local, gv_local = back(queries, keys, values, ga, incoming, first)
    gk, gv = finish(keys, values, gk_local, gv_local, arriving, last)
    return normed, gq, gk, gv


def solution(mesh):
    spec = P("ctx", "head")
    return jax.shard_map(
        on_device,
        mesh=mesh,
        in_specs=(spec, spec, spec, P("head"), spec),
        out_specs=(spec,) * 4,
        check_vma=False,
    )
```

```python
import jax
import jax.numpy as jnp
from jax import lax
from jax.experimental import pallas as pl
from jax.experimental.pallas import tpu as pltpu
from jax.sharding import PartitionSpec as P

HEAD_DIM = 128
GROUP = 512
HALF = 256
EPSILON = 1e-06
CTX = 32
HEADS_LOCAL = 4
F32 = jnp.float32
BF16 = jnp.bfloat16


NT = (((1,), (1,)), ((), ()))
TN = (((0,), (0,)), ((), ()))
NN = (((1,), (0,)), ((), ()))


def mm(a, b, dims):
    return lax.dot_general(a, b, dims, preferred_element_type=F32)


def mm_exact(a, b, dims):
    return lax.dot_general(a, b, dims, preferred_element_type=F32, precision=lax.Precision.HIGHEST)


def causal(rows, cols, row0, col0, flip):
    t = lax.broadcasted_iota(jnp.int32, (rows, cols), 0) + row0
    s = lax.broadcasted_iota(jnp.int32, (rows, cols), 1) + col0
    return (s >= t) if flip else (t >= s)


WIDE = 60 << 20
LARGE = 44 << 20
BIG_BF16 = (21504, 512)
BIG_F32 = (10752, 512)
BIG_LAST = (43008, 128)


def call(kernel, in_specs, out_specs, out_shape, grid=(), scratch=(), flops=0, nbytes=0, vmem=16 << 20):
    return pl.pallas_call(
        kernel,
        grid=grid,
        in_specs=in_specs,
        out_specs=out_specs,
        out_shape=out_shape,
        scratch_shapes=list(scratch),
        compiler_params=pltpu.CompilerParams(vmem_limit_bytes=vmem),
        cost_estimate=pl.CostEstimate(flops=flops, bytes_accessed=nbytes, transcendentals=0),
    )


VMEM = pl.BlockSpec(memory_space=pltpu.VMEM)
ANY = pl.BlockSpec(memory_space=pl.ANY)


def struct(shape, dtype):
    return jax.ShapeDtypeStruct(shape, dtype)


def moment_kernel(k_ref, v_ref, total_ref, first_ref):
    first = mm(k_ref[:GROUP], v_ref[:GROUP], TN)
    second = mm(k_ref[GROUP:], v_ref[GROUP:], TN)
    first_ref[...] = first
    total_ref[...] = first + second


def moments(k, v):
    spec = pl.BlockSpec((2 * GROUP, HEAD_DIM), lambda h: (0, h))
    out = pl.BlockSpec((HEAD_DIM, HEAD_DIM), lambda h: (h, 0))
    return call(
        moment_kernel,
        [spec, spec],
        [out, out],
        [struct((512, 128), F32)] * 2,
        grid=(HEADS_LOCAL,),
        flops=8 * 2 * 512 * 128 * 128,
        nbytes=2 << 20,
        vmem=WIDE,
    )(k, v)


def local_kernel(q_ref, k_ref, v_ref, out_ref, early_ref, late_ref):
    for r in (0, 1):
        n = HALF * (r + 1)
        rows = pl.ds(r * HALF, HALF)
        scores = mm(q_ref[rows], k_ref[:n], NT)
        probs = jnp.where(causal(HALF, n, r * HALF, 0, False), scores, 0.0).astype(BF16)
        out_ref[rows] = mm(probs, v_ref[:n], NN)
    for c, flipped_ref in ((0, early_ref), (1, late_ref)):
        rows = pl.ds(c * HALF, HALF)
        rest = pl.ds(c * HALF, GROUP - c * HALF)
        mask = causal(HALF, GROUP - c * HALF, 0, 0, True)
        flipped_ref[...] = jnp.where(mask, mm(k_ref[rows], q_ref[rest], NT), 0.0).astype(BF16)


def local_attention(q, k, v):
    spec = pl.BlockSpec((GROUP, HEAD_DIM), lambda h, j: (j, h))
    early = pl.BlockSpec((HALF, GROUP), lambda h, j: (2 * h + j, 0))
    late = pl.BlockSpec((HALF, HALF), lambda h, j: (2 * h + j, 0))
    return call(
        local_kernel,
        [spec] * 3,
        [spec, early, late],
        [struct(BIG_F32, F32), struct((2048, 512), BF16), struct((2048, 256), BF16)],
        grid=(HEADS_LOCAL, 2),
        flops=8 * 3 * 2 * 512 * 512 * 128,
        nbytes=8 << 20,
        vmem=WIDE,
    )(q, k, v)


def picker(c):
    row = lax.broadcasted_iota(jnp.int32, (16, 256), 0)
    lane = lax.broadcasted_iota(jnp.int32, (16, 256), 1)
    return jnp.where(row == jnp.where(lane >= 128, 2 * c + 1, 2 * c), 1.0, 0.0).astype(F32)


def attend_kernel(q_ref, local_ref, g_ref, gain_ref, incoming_ref, first_ref, att_ref, stats_ref, buf, sems):
    copies = []
    for i in range(4):
        tokens = pl.ds(i * HALF, HALF)
        copy = pltpu.make_async_copy(local_ref.at[tokens], buf.at[tokens], sems.at[i])
        copy.start()
        copies.append(copy)
    sums = jnp.zeros((16, 128), F32)
    for j in (0, 1):
        states = []
        for h in range(HEADS_LOCAL):
            rows = pl.ds(h * HEAD_DIM, HEAD_DIM)
            state = incoming_ref[rows] + first_ref[rows] if j else incoming_ref[rows]
            states.append(state.astype(BF16))
        for i in (2 * j, 2 * j + 1):
            tokens = pl.ds(i * HALF, HALF)
            square = inner = None
            copies[i].wait()
            for h in range(HEADS_LOCAL):
                cols = pl.ds(h * HEAD_DIM, HEAD_DIM)
                att = mm(q_ref[tokens, cols], states[h], NN) + buf[tokens, cols]
                att_ref[tokens, cols] = att
                dot = gain_ref[:, cols] * g_ref[tokens, cols].astype(F32) * att
                square = att * att if h == 0 else square + att * att
                inner = dot if h == 0 else inner + dot
            both = jnp.concatenate([square, inner], axis=1)
            for c in (0, 1):
                sums = sums + mm_exact(picker(2 * i + c), both[c * 128 : (c + 1) * 128], NT)
    stats_ref[...] = jnp.broadcast_to(sums[None], stats_ref.shape)


def attend(q, local, g, gain, incoming, first):
    return call(
        attend_kernel,
        [VMEM, ANY] + [VMEM] * 4,
        [VMEM] * 2,
        [struct((1024, 512), F32), struct((8, 16, 128), F32)],
        scratch=[pltpu.VMEM((1024, 512), F32), pltpu.SemaphoreType.DMA((4,))],
        flops=2 * 1024 * 512 * 128,
        nbytes=6 << 20,
        vmem=LARGE,
    )(q, local, g, gain, incoming, first)


def norm_kernel(att_ref, g_ref, q_ref, gain_ref, stats_ref, normed_ref, ga_ref, total_ref, last_ref, nbuf, gbuf, lbuf, sems, lsem):
    sums = jnp.sum(stats_ref[...], axis=0)
    total = [None] * HEADS_LOCAL
    copies = []
    for i in range(4):
        tokens = pl.ds(i * HALF, HALF)
        wide = jnp.concatenate([mm_exact(sums, picker(2 * i + c), TN) for c in (0, 1)], axis=0)
        inverse = 1.0 / jnp.sqrt(wide[:, :128] * (1.0 / 4096) + EPSILON)
        mean = wide[:, 128:] * inverse * (1.0 / 4096)
        for h in range(HEADS_LOCAL):
            cols = pl.ds(h * HEAD_DIM, HEAD_DIM)
            gain = gain_ref[:, cols]
            unit = att_ref[tokens, cols] * inverse
            nbuf[tokens, cols] = (unit * gain).astype(BF16)
            ga = ((gain * g_ref[tokens, cols].astype(F32) - unit * mean) * inverse).astype(BF16)
            gbuf[tokens, cols] = ga
            part = mm(q_ref[tokens, cols], ga, TN)
            if i == 2:
                first = total[h]
                total[h] = part
            elif i == 0:
                total[h] = part
            else:
                total[h] = total[h] + part
            rows = pl.ds(h * HEAD_DIM, HEAD_DIM)
            if i == 1:
                total_ref[rows] = total[h]
            if i == 3:
                lbuf[rows] = total[h]
                total_ref[rows] += total[h]
        for n, (buf, out) in enumerate(((nbuf, normed_ref), (gbuf, ga_ref))):
            copy = pltpu.make_async_copy(buf.at[tokens], out.at[tokens], sems.at[n, i])
            copy.start()
            copies.append(copy)
    copy = pltpu.make_async_copy(lbuf, last_ref.at[pl.ds(0, 512)], lsem)
    copy.start()
    copies.append(copy)
    for copy in copies:
        copy.wait()


def norm(att, g, q, gain, stats):
    return call(
        norm_kernel,
        [VMEM] * 5,
        [ANY, ANY, VMEM, ANY],
        [struct((1024, 512), BF16), struct(BIG_BF16, BF16), struct((512, 128), F32), struct(BIG_LAST, F32)],
        scratch=[pltpu.VMEM((1024, 512), BF16)] * 2
        + [pltpu.VMEM((512, 128), F32), pltpu.SemaphoreType.DMA((2, 4)), pltpu.SemaphoreType.DMA],
        flops=2 * 1024 * 512 * 128,
        nbytes=6 << 20,
        vmem=LARGE,
    )(att, g, q, gain, stats)


def back_kernel(q_ref, k_ref, v_ref, ga_ref, early_ref, late_ref, incoming_ref, first_ref, gq_ref, gk_ref, gv_ref):
    second = pl.program_id(1) == 1
    state = (incoming_ref[...] + jnp.where(second, first_ref[...], 0.0)).astype(BF16)
    for r in (0, 1):
        n = HALF * (r + 1)
        rows = pl.ds(r * HALF, HALF)
        grads = mm(ga_ref[rows], v_ref[:n], NT)
        grads = jnp.where(causal(HALF, n, r * HALF, 0, False), grads, 0.0).astype(BF16)
        gq = mm(ga_ref[rows], state, NT) + mm(grads, k_ref[:n], NN)
        gq_ref[rows] = gq.astype(BF16)
    for c, flipped_ref in ((0, early_ref), (1, late_ref)):
        rows = pl.ds(c * HALF, HALF)
        rest = pl.ds(c * HALF, GROUP - c * HALF)
        mask = causal(HALF, GROUP - c * HALF, 0, 0, True)
        grads = jnp.where(mask, mm(v_ref[rows], ga_ref[rest], NT), 0.0).astype(BF16)
        gk_ref[rows] = mm(grads, q_ref[rest], NN)
        gv_ref[rows] = mm(flipped_ref[...], ga_ref[rest], NN)


def back(q, k, v, ga, early, late, incoming, first):
    spec = pl.BlockSpec((GROUP, HEAD_DIM), lambda h, j: (j, h))
    state = pl.BlockSpec((HEAD_DIM, HEAD_DIM), lambda h, j: (h, 0))
    flipped = [pl.BlockSpec((HALF, n), lambda h, j: (2 * h + j, 0)) for n in (GROUP, HALF)]
    return call(
        back_kernel,
        [spec] * 4 + flipped + [state] * 2,
        [spec] * 3,
        [struct((1024, 512), BF16), struct(BIG_F32, F32), struct(BIG_F32, F32)],
        grid=(HEADS_LOCAL, 2),
        flops=8 * 5 * 2 * 512 * 512 * 128,
        nbytes=12 << 20,
        vmem=WIDE,
    )(q, k, v, ga, early, late, incoming, first)


def last_kernel(
    k_ref, v_ref, gkl_ref, gvl_ref, arriving_ref, last_hbm, gk_ref, gv_ref, klocal, vlocal, kbuf, vbuf, last_ref, insems, sems, lsem
):
    last_copy = pltpu.make_async_copy(last_hbm.at[pl.ds(0, 512)], last_ref, lsem)
    last_copy.start()
    arrivals = []
    for j in (0, 1):
        tokens = pl.ds(j * GROUP, GROUP)
        for n, (src, buf) in enumerate(((gkl_ref, klocal), (gvl_ref, vlocal))):
            copy = pltpu.make_async_copy(src.at[tokens], buf.at[tokens], insems.at[n, j])
            copy.start()
            arrivals.append(copy)
    copies = []
    last_copy.wait()
    for j in (0, 1):
        tokens = pl.ds(j * GROUP, GROUP)
        suffixes = []
        for h in range(HEADS_LOCAL):
            rows = pl.ds(h * HEAD_DIM, HEAD_DIM)
            suffix = arriving_ref[rows] if j else arriving_ref[rows] + last_ref[rows]
            suffixes.append(suffix.astype(BF16))
        for n, (x_ref, local, buf, out, dims) in enumerate(
            ((v_ref, klocal, kbuf, gk_ref, NT), (k_ref, vlocal, vbuf, gv_ref, NN))
        ):
            arrivals[2 * j + n].wait()
            for h in range(HEADS_LOCAL):
                cols = pl.ds(h * HEAD_DIM, HEAD_DIM)
                buf[tokens, cols] = (mm(x_ref[tokens, cols], suffixes[h], dims) + local[tokens, cols]).astype(BF16)
            copy = pltpu.make_async_copy(buf.at[tokens], out.at[tokens], sems.at[n, j])
            copy.start()
            copies.append(copy)
    for copy in copies:
        copy.wait()


def finish(k, v, gk_local, gv_local, arriving, last):
    return call(
        last_kernel,
        [VMEM, VMEM, ANY, ANY, VMEM, ANY],
        [ANY] * 2,
        [struct((1024, 512), BF16)] * 2,
        scratch=[pltpu.VMEM((1024, 512), F32)] * 2
        + [pltpu.VMEM((1024, 512), BF16)] * 2
        + [pltpu.VMEM((512, 128), F32)]
        + [pltpu.SemaphoreType.DMA((2, 2))] * 2
        + [pltpu.SemaphoreType.DMA],
        flops=2 * 2 * 1024 * 512 * 128,
        nbytes=8 << 20,
        vmem=LARGE,
    )(k, v, gk_local, gv_local, arriving, last)


def running(pieces, after, reverse):
    def kernel(pieces_ref, after_ref, out_ref):
        run = jnp.zeros(pieces_ref.shape[1:], F32)
        order = range(CTX - 1, -1, -1) if reverse else range(CTX)
        for i in order:
            out_ref[i] = run
            run = run + pieces_ref[i]

    return call(kernel, [VMEM, ANY], VMEM, struct(pieces.shape, F32), flops=1 << 17, nbytes=1 << 19, vmem=LARGE)(
        pieces, after
    )


def exchange(value):
    return lax.all_to_all(value, "ctx", 0, 0, tiled=True)


def split(total):
    return exchange(total.reshape(CTX, 512 // CTX, 128))


def merge(sums):
    return exchange(sums).reshape(512, 128)


def on_device(queries, keys, values, gain, grad_normed):
    gain = gain.reshape(1, 512)
    total, first = moments(keys, values)
    pieces = split(total)
    local, early, late = local_attention(queries, keys, values)
    incoming = merge(running(pieces, local, False))
    att, stats = attend(queries, local, grad_normed, gain, incoming, first)
    stats = lax.all_to_all(stats, "head", 0, 0, tiled=True)
    normed, ga, cototal, last = norm(att, grad_normed, queries, gain, stats)
    pieces = split(cototal)
    gq, gk_local, gv_local = back(queries, keys, values, ga, early, late, incoming, first)
    arriving = merge(running(pieces, gk_local, True))
    gk, gv = finish(keys, values, gk_local, gv_local, arriving, last)
    return normed, gq, gk, gv


def solution(mesh):
    spec = P("ctx", "head")
    return jax.shard_map(
        on_device,
        mesh=mesh,
        in_specs=(spec, spec, spec, P("head"), spec),
        out_specs=(spec,) * 4,
        check_vma=False,
    )
```

```python
import jax
import jax.numpy as jnp
from jax import lax
from jax.experimental import pallas as pl
from jax.experimental.pallas import tpu as pltpu
from jax.sharding import PartitionSpec as P

HEAD_DIM = 128
GROUP = 512
HALF = 256
EPSILON = 1e-06
CTX = 32
HEADS_LOCAL = 4
F32 = jnp.float32
BF16 = jnp.bfloat16


NT = (((1,), (1,)), ((), ()))
TN = (((0,), (0,)), ((), ()))
NN = (((1,), (0,)), ((), ()))


def mm(a, b, dims):
    return lax.dot_general(a, b, dims, preferred_element_type=F32)


def terms(x, count):
    out = []
    for _ in range(count - 1):
        high = x.astype(BF16)
        out.append(high)
        x = x - high.astype(F32)
    return out + [x.astype(BF16)]


def triangle(flip):
    row = lax.broadcasted_iota(jnp.int32, (HALF, HALF), 0)
    col = lax.broadcasted_iota(jnp.int32, (HALF, HALF), 1)
    return (col >= row) if flip else (row >= col)


def diagonal(stacked):
    half = stacked.astype(BF16)
    upper = lax.broadcasted_iota(jnp.int32, half.shape, 0) < HEAD_DIM
    zero = jnp.zeros_like(half)
    return jnp.concatenate([jnp.where(upper, half, zero), jnp.where(upper, zero, half)], axis=1)


def side_by_side(a, b):
    return jnp.concatenate([a, b], axis=1)


WIDE = 60 << 20
LARGE = 44 << 20
BIG_BF16 = (21504, 512)
BIG_F32 = (10752, 512)
BIG_LAST = (43008, 128)


def call(kernel, in_specs, out_specs, out_shape, grid=(), scratch=(), flops=0, nbytes=0, vmem=16 << 20):
    return pl.pallas_call(
        kernel,
        grid=grid,
        in_specs=in_specs,
        out_specs=out_specs,
        out_shape=out_shape,
        scratch_shapes=list(scratch),
        compiler_params=pltpu.CompilerParams(vmem_limit_bytes=vmem),
        cost_estimate=pl.CostEstimate(flops=flops, bytes_accessed=nbytes, transcendentals=0),
    )


VMEM = pl.BlockSpec(memory_space=pltpu.VMEM)
ANY = pl.BlockSpec(memory_space=pl.ANY)


def struct(shape, dtype):
    return jax.ShapeDtypeStruct(shape, dtype)


def moment_kernel(k_ref, v_ref, total_ref, first_ref):
    first = mm(k_ref[:GROUP], v_ref[:GROUP], TN)
    second = mm(k_ref[GROUP:], v_ref[GROUP:], TN)
    first_ref[...] = first
    total_ref[...] = first + second


def moments(k, v):
    spec = pl.BlockSpec((2 * GROUP, HEAD_DIM), lambda h: (0, h))
    out = pl.BlockSpec((HEAD_DIM, HEAD_DIM), lambda h: (h, 0))
    return call(
        moment_kernel,
        [spec, spec],
        [out, out],
        [struct((512, 128), F32)] * 2,
        grid=(HEADS_LOCAL,),
        flops=8 * 2 * 512 * 128 * 128,
        nbytes=2 << 20,
        vmem=WIDE,
    )(k, v)


def local_kernel(q_ref, k_ref, v_ref, out_ref, early_ref, late_ref, flip_ref):
    lower, upper = triangle(False), triangle(True)
    for j in (0, 1):
        one, two = pl.ds(j * GROUP, HALF), pl.ds(j * GROUP + HALF, HALF)
        both = pl.ds(j * GROUP, GROUP)
        probs = jnp.where(lower, mm(q_ref[one], k_ref[one], NT), 0.0).astype(BF16)
        out_ref[one] = mm(probs, v_ref[one], NN)
        probs = side_by_side(
            mm(q_ref[two], k_ref[one], NT).astype(BF16),
            jnp.where(lower, mm(q_ref[two], k_ref[two], NT), 0.0).astype(BF16),
        )
        out_ref[two] = mm(probs, v_ref[both], NN)
        rows = pl.ds(j * HALF, HALF)
        early_ref[rows, :HALF] = jnp.where(upper, mm(k_ref[one], q_ref[one], NT), 0.0).astype(BF16)
        early_ref[rows, HALF:] = mm(k_ref[one], q_ref[two], NT).astype(BF16)
        late_ref[rows] = jnp.where(upper, mm(k_ref[two], q_ref[two], NT), 0.0).astype(BF16)
        flip_ref[:, both] = jnp.transpose(q_ref[both], (1, 0))


def local_attention(q, k, v):
    spec = pl.BlockSpec((2 * GROUP, HEAD_DIM), lambda h: (0, h))
    return call(
        local_kernel,
        [spec] * 3,
        [spec]
        + [pl.BlockSpec((GROUP, n), lambda h: (h, 0)) for n in (GROUP, HALF)]
        + [pl.BlockSpec((HEAD_DIM, 1024), lambda h: (h, 0))],
        [struct(BIG_F32, F32), struct((2048, 512), BF16), struct((2048, 256), BF16), struct((512, 1024), BF16)],
        grid=(HEADS_LOCAL,),
        flops=8 * 3 * 2 * 512 * 512 * 128,
        nbytes=9 << 20,
        vmem=WIDE,
    )(q, k, v)


def picker(i, copies):
    row = lax.broadcasted_iota(jnp.int32, (8 * copies, HALF), 0) & 7
    lane = lax.broadcasted_iota(jnp.int32, (8 * copies, HALF), 1)
    return jnp.where(row == jnp.where(lane >= 128, 2 * i + 1, 2 * i), 1.0, 0.0).astype(BF16)


def attend_kernel(q_ref, local_ref, g_ref, gain_ref, incoming_ref, first_ref, att_ref, stats_ref, buf, sems):
    copies = []
    for i in range(4):
        tokens = pl.ds(i * HALF, HALF)
        copy = pltpu.make_async_copy(local_ref.at[tokens], buf.at[tokens], sems.at[i])
        copy.start()
        copies.append(copy)
    sums = jnp.zeros((8, HALF), F32)
    for j in (0, 1):
        states = []
        for p in (0, 1):
            rows = pl.ds(p * 256, 256)
            states.append(diagonal(incoming_ref[rows] + first_ref[rows] if j else incoming_ref[rows]))
        for i in (2 * j, 2 * j + 1):
            tokens = pl.ds(i * HALF, HALF)
            square = inner = 0.0
            copies[i].wait()
            for p in (0, 1):
                cols = pl.ds(p * 256, 256)
                att = mm(q_ref[tokens, cols], states[p], NN) + buf[tokens, cols]
                att_ref[tokens, cols] = att
                dot = gain_ref[:, cols] * g_ref[tokens, cols].astype(F32) * att
                att = att * att
                square = square + att[:, :128] + att[:, 128:]
                inner = inner + dot[:, :128] + dot[:, 128:]
            for term in terms(side_by_side(square, inner), 2):
                sums = sums + mm(picker(i, 1), term, NT)
    stats_ref[...] = jnp.broadcast_to(sums[None], stats_ref.shape)


def attend(q, local, g, gain, incoming, first):
    return call(
        attend_kernel,
        [VMEM, ANY] + [VMEM] * 4,
        [VMEM] * 2,
        [struct((1024, 512), F32), struct((8, 8, HALF), F32)],
        scratch=[pltpu.VMEM((1024, 512), F32), pltpu.SemaphoreType.DMA((4,))],
        flops=2 * 1024 * 512 * 128,
        nbytes=6 << 20,
        vmem=LARGE,
    )(q, local, g, gain, incoming, first)


def norm_kernel(att_ref, g_ref, flip_ref, gain_ref, stats_ref, normed_ref, ga_ref, total_ref, last_ref, nbuf, gbuf, lbuf, sems, lsem):
    sums = jnp.concatenate(terms(jnp.sum(stats_ref[...], axis=0), 3), axis=0)
    copies = []
    for j in (0, 1):
        both = pl.ds(j * GROUP, GROUP)
        for i in (2 * j, 2 * j + 1):
            tokens = pl.ds(i * HALF, HALF)
            wide = mm(sums, picker(i, 3), TN)
            inverse = lax.rsqrt(wide[:, :128] * (1.0 / 4096) + EPSILON)
            mean = wide[:, 128:] * inverse * (1.0 / 4096)
            for h in range(HEADS_LOCAL):
                cols = pl.ds(h * HEAD_DIM, HEAD_DIM)
                gain = gain_ref[:, cols]
                unit = att_ref[tokens, cols] * inverse
                nbuf[tokens, cols] = (unit * gain).astype(BF16)
                gbuf[tokens, cols] = ((gain * g_ref[tokens, cols].astype(F32) - unit * mean) * inverse).astype(BF16)
        for n, (buf, out) in enumerate(((nbuf, normed_ref), (gbuf, ga_ref))):
            copy = pltpu.make_async_copy(buf.at[both], out.at[both], sems.at[n, j])
            copy.start()
            copies.append(copy)
        for h in range(HEADS_LOCAL):
            rows = pl.ds(h * HEAD_DIM, HEAD_DIM)
            part = mm(flip_ref[rows, both], gbuf[both, rows], NN)
            if j == 0:
                total_ref[rows] = part
            else:
                lbuf[rows] = part
                total_ref[rows] += part
    copy = pltpu.make_async_copy(lbuf, last_ref.at[pl.ds(0, 512)], lsem)
    copy.start()
    copies.append(copy)
    for copy in copies:
        copy.wait()


def norm(att, g, flip, gain, stats):
    return call(
        norm_kernel,
        [VMEM] * 5,
        [ANY, ANY, VMEM, ANY],
        [struct((1024, 512), BF16), struct(BIG_BF16, BF16), struct((512, 128), F32), struct(BIG_LAST, F32)],
        scratch=[pltpu.VMEM((1024, 512), BF16)] * 2
        + [pltpu.VMEM((512, 128), F32), pltpu.SemaphoreType.DMA((2, 2)), pltpu.SemaphoreType.DMA],
        flops=2 * 1024 * 512 * 128,
        nbytes=6 << 20,
        vmem=LARGE,
    )(att, g, flip, gain, stats)


def back_kernel(q_ref, v_ref, ga_ref, early_ref, late_ref, gk_ref, gv_ref):
    upper = triangle(True)
    for j in (0, 1):
        one, two = pl.ds(j * GROUP, HALF), pl.ds(j * GROUP + HALF, HALF)
        both = pl.ds(j * GROUP, GROUP)
        rows = pl.ds(j * HALF, HALF)
        grads = side_by_side(
            jnp.where(upper, mm(v_ref[one], ga_ref[one], NT), 0.0).astype(BF16),
            mm(v_ref[one], ga_ref[two], NT).astype(BF16),
        )
        gk_ref[one] = mm(grads, q_ref[both], NN)
        grads = jnp.where(upper, mm(v_ref[two], ga_ref[two], NT), 0.0).astype(BF16)
        gk_ref[two] = mm(grads, q_ref[two], NN)
        gv_ref[one] = mm(early_ref[rows], ga_ref[both], NN)
        gv_ref[two] = mm(late_ref[rows], ga_ref[two], NN)


def back(q, v, ga, early, late):
    spec = pl.BlockSpec((2 * GROUP, HEAD_DIM), lambda h: (0, h))
    return call(
        back_kernel,
        [spec] * 3 + [pl.BlockSpec((GROUP, n), lambda h: (h, 0)) for n in (GROUP, HALF)],
        [spec] * 2,
        [struct(BIG_F32, F32), struct(BIG_F32, F32)],
        grid=(HEADS_LOCAL,),
        flops=8 * 3 * 2 * 512 * 512 * 128,
        nbytes=10 << 20,
        vmem=WIDE,
    )(q, v, ga, early, late)


def query_kernel(k_ref, v_ref, ga_ref, incoming_ref, first_ref, gq_ref):
    lower = triangle(False)
    for j in (0, 1):
        one, two = pl.ds(j * GROUP, HALF), pl.ds(j * GROUP + HALF, HALF)
        both = pl.ds(j * GROUP, GROUP)
        state = (incoming_ref[...] + first_ref[...] if j else incoming_ref[...]).astype(BF16)
        grads = jnp.where(lower, mm(ga_ref[one], v_ref[one], NT), 0.0).astype(BF16)
        gq_ref[one] = (mm(ga_ref[one], state, NT) + mm(grads, k_ref[one], NN)).astype(BF16)
        grads = side_by_side(
            mm(ga_ref[two], v_ref[one], NT).astype(BF16),
            jnp.where(lower, mm(ga_ref[two], v_ref[two], NT), 0.0).astype(BF16),
        )
        gq_ref[two] = (mm(ga_ref[two], state, NT) + mm(grads, k_ref[both], NN)).astype(BF16)


def query_grad(k, v, ga, incoming, first):
    spec = pl.BlockSpec((2 * GROUP, HEAD_DIM), lambda h: (0, h))
    state = pl.BlockSpec((HEAD_DIM, HEAD_DIM), lambda h: (h, 0))
    return call(
        query_kernel,
        [spec] * 3 + [state] * 2,
        spec,
        struct((1024, 512), BF16),
        grid=(HEADS_LOCAL,),
        flops=8 * 2 * 2 * 512 * 512 * 128,
        nbytes=5 << 20,
        vmem=WIDE,
    )(k, v, ga, incoming, first)


def last_kernel(
    k_ref, v_ref, gkl_ref, gvl_ref, arriving_ref, last_hbm, gk_ref, gv_ref, klocal, vlocal, kbuf, vbuf, last_ref, insems, sems, lsem
):
    last_copy = pltpu.make_async_copy(last_hbm.at[pl.ds(0, 512)], last_ref, lsem)
    arrivals = {}
    for j in (1, 0):
        tokens = pl.ds(j * GROUP, GROUP)
        for n, (src, buf) in enumerate(((gkl_ref, klocal), (gvl_ref, vlocal))):
            arrivals[n, j] = pltpu.make_async_copy(src.at[tokens], buf.at[tokens], insems.at[n, j])
            arrivals[n, j].start()
        if j:
            last_copy.start()
    copies = []
    for j in (1, 0):
        tokens = pl.ds(j * GROUP, GROUP)
        suffixes = []
        if not j:
            last_copy.wait()
        for p in (0, 1):
            rows = pl.ds(p * 256, 256)
            suffixes.append(diagonal(arriving_ref[rows] if j else arriving_ref[rows] + last_ref[rows]))
        for n, (x_ref, local, buf, out, dims) in enumerate(
            ((v_ref, klocal, kbuf, gk_ref, NT), (k_ref, vlocal, vbuf, gv_ref, NN))
        ):
            products = [mm(x_ref[tokens, pl.ds(p * 256, 256)], suffixes[p], dims) for p in (0, 1)]
            arrivals[n, j].wait()
            for p in (0, 1):
                cols = pl.ds(p * 256, 256)
                buf[tokens, cols] = (products[p] + local[tokens, cols]).astype(BF16)
            copy = pltpu.make_async_copy(buf.at[tokens], out.at[tokens], sems.at[n, j])
            copy.start()
            copies.append(copy)
    for copy in copies:
        copy.wait()


def finish(k, v, gk_local, gv_local, arriving, last):
    return call(
        last_kernel,
        [VMEM, VMEM, ANY, ANY, VMEM, ANY],
        [ANY] * 2,
        [struct((1024, 512), BF16)] * 2,
        scratch=[pltpu.VMEM((1024, 512), F32)] * 2
        + [pltpu.VMEM((1024, 512), BF16)] * 2
        + [pltpu.VMEM((512, 128), F32)]
        + [pltpu.SemaphoreType.DMA((2, 2))] * 2
        + [pltpu.SemaphoreType.DMA],
        flops=2 * 2 * 1024 * 512 * 128,
        nbytes=8 << 20,
        vmem=LARGE,
    )(k, v, gk_local, gv_local, arriving, last)


def running(pieces, after, reverse):
    def kernel(pieces_ref, after_ref, out_ref):
        run = jnp.zeros(pieces_ref.shape[1:], F32)
        order = range(CTX - 1, -1, -1) if reverse else range(CTX)
        for i in order:
            out_ref[i] = run
            run = run + pieces_ref[i]

    return call(kernel, [VMEM, ANY], VMEM, struct(pieces.shape, F32), flops=1 << 17, nbytes=1 << 19, vmem=LARGE)(
        pieces, after
    )


def exchange(value):
    return lax.all_to_all(value, "ctx", 0, 0, tiled=True)


def split(total):
    return exchange(total.reshape(CTX, 512 // CTX, 128))


def merge(sums):
    return exchange(sums).reshape(512, 128)


def on_device(queries, keys, values, gain, grad_normed):
    gain = gain.reshape(1, 512)
    total, first = moments(keys, values)
    pieces = split(total)
    local, early, late, flip = local_attention(queries, keys, values)
    incoming = merge(running(pieces, local, False))
    att, stats = attend(queries, local, grad_normed, gain, incoming, first)
    stats = lax.all_to_all(stats, "head", 0, 0, tiled=True)
    normed, ga, cototal, last = norm(att, grad_normed, flip, gain, stats)
    pieces = split(cototal)
    gk_local, gv_local = back(queries, values, ga, early, late)
    arriving = merge(running(pieces, gk_local, True))
    gq = query_grad(keys, values, ga, incoming, first)
    gk, gv = finish(keys, values, gk_local, gv_local, arriving, last)
    return normed, gq, gk, gv


def solution(mesh):
    spec = P("ctx", "head")
    return jax.shard_map(
        on_device,
        mesh=mesh,
        in_specs=(spec, spec, spec, P("head"), spec),
        out_specs=(spec,) * 4,
        check_vma=False,
    )
```

```python
import jax
import jax.numpy as jnp
from jax import lax
from jax.experimental import pallas as pl
from jax.experimental.pallas import tpu as pltpu
from jax.sharding import PartitionSpec as P

HEAD_DIM = 128
GROUP = 512
HALF = 256
EPSILON = 1e-06
CTX = 32
HEADS_LOCAL = 4
F32 = jnp.float32
BF16 = jnp.bfloat16


NT = (((1,), (1,)), ((), ()))
TN = (((0,), (0,)), ((), ()))
NN = (((1,), (0,)), ((), ()))


def mm(a, b, dims):
    return lax.dot_general(a, b, dims, preferred_element_type=F32)


def terms(x, count):
    out = []
    for _ in range(count - 1):
        high = x.astype(BF16)
        out.append(high)
        x = x - high.astype(F32)
    return out + [x.astype(BF16)]


def triangle(flip):
    row = lax.broadcasted_iota(jnp.int32, (HALF, HALF), 0)
    col = lax.broadcasted_iota(jnp.int32, (HALF, HALF), 1)
    return (col >= row) if flip else (row >= col)


def diagonal(stacked):
    half = stacked.astype(BF16)
    upper = lax.broadcasted_iota(jnp.int32, half.shape, 0) < HEAD_DIM
    zero = jnp.zeros_like(half)
    return jnp.concatenate([jnp.where(upper, half, zero), jnp.where(upper, zero, half)], axis=1)


def side_by_side(a, b):
    return jnp.concatenate([a, b], axis=1)


WIDE = 60 << 20
LARGE = 44 << 20
BIG_BF16 = (21504, 512)
BIG_F32 = (10752, 512)
BIG_LAST = (43008, 128)


def call(kernel, in_specs, out_specs, out_shape, grid=(), scratch=(), flops=0, nbytes=0, vmem=16 << 20):
    return pl.pallas_call(
        kernel,
        grid=grid,
        in_specs=in_specs,
        out_specs=out_specs,
        out_shape=out_shape,
        scratch_shapes=list(scratch),
        compiler_params=pltpu.CompilerParams(vmem_limit_bytes=vmem),
        cost_estimate=pl.CostEstimate(flops=flops, bytes_accessed=nbytes, transcendentals=0),
    )


VMEM = pl.BlockSpec(memory_space=pltpu.VMEM)
ANY = pl.BlockSpec(memory_space=pl.ANY)


def struct(shape, dtype):
    return jax.ShapeDtypeStruct(shape, dtype)


def moment_kernel(k_hbm, v_hbm, total_ref, first_ref, k_ref, v_ref, sems):
    copies = []
    for i in range(4):
        tokens = pl.ds(i * HALF, HALF)
        for n, (src, buf) in enumerate(((k_hbm, k_ref), (v_hbm, v_ref))):
            copy = pltpu.make_async_copy(src.at[tokens], buf.at[tokens], sems.at[n, i])
            copy.start()
            copies.append(copy)
    for j in (0, 1):
        sums = [0.0, 0.0]
        for i in (2 * j, 2 * j + 1):
            tokens = pl.ds(i * HALF, HALF)
            copies[2 * i].wait()
            copies[2 * i + 1].wait()
            for p in (0, 1):
                cols = pl.ds(p * 256, 256)
                sums[p] = sums[p] + mm(k_ref[tokens, cols], v_ref[tokens, cols], TN)
        for p in (0, 1):
            for n in (0, 1):
                rows = pl.ds(p * 256 + n * 128, 128)
                part = sums[p][n * 128 : n * 128 + 128, n * 128 : n * 128 + 128]
                if j == 0:
                    first_ref[rows] = part
                else:
                    total_ref[rows] = first_ref[rows] + part


def moments(k, v):
    return call(
        moment_kernel,
        [ANY] * 2,
        [VMEM] * 2,
        [struct((512, 128), F32)] * 2,
        scratch=[pltpu.VMEM((1024, 512), BF16)] * 2 + [pltpu.SemaphoreType.DMA((2, 4))],
        flops=8 * 2 * 512 * 128 * 128,
        nbytes=2 << 20,
        vmem=WIDE,
    )(k, v)


def local_kernel(q_ref, k_ref, v_ref, out_ref, early_ref, late_ref, flip_ref):
    lower, upper = triangle(False), triangle(True)
    for j in (0, 1):
        one, two = pl.ds(j * GROUP, HALF), pl.ds(j * GROUP + HALF, HALF)
        both = pl.ds(j * GROUP, GROUP)
        probs = jnp.where(lower, mm(q_ref[one], k_ref[one], NT), 0.0).astype(BF16)
        out_ref[one] = mm(probs, v_ref[one], NN)
        probs = side_by_side(
            mm(q_ref[two], k_ref[one], NT).astype(BF16),
            jnp.where(lower, mm(q_ref[two], k_ref[two], NT), 0.0).astype(BF16),
        )
        out_ref[two] = mm(probs, v_ref[both], NN)
        rows = pl.ds(j * HALF, HALF)
        early_ref[rows, :HALF] = jnp.where(upper, mm(k_ref[one], q_ref[one], NT), 0.0).astype(BF16)
        early_ref[rows, HALF:] = mm(k_ref[one], q_ref[two], NT).astype(BF16)
        late_ref[rows] = jnp.where(upper, mm(k_ref[two], q_ref[two], NT), 0.0).astype(BF16)
        flip_ref[:, both] = jnp.transpose(q_ref[both], (1, 0))


def local_attention(q, k, v):
    spec = pl.BlockSpec((2 * GROUP, HEAD_DIM), lambda h: (0, h))
    return call(
        local_kernel,
        [spec] * 3,
        [spec]
        + [pl.BlockSpec((GROUP, n), lambda h: (h, 0)) for n in (GROUP, HALF)]
        + [pl.BlockSpec((HEAD_DIM, 1024), lambda h: (h, 0))],
        [struct(BIG_F32, F32), struct((2048, 512), BF16), struct((2048, 256), BF16), struct((512, 1024), BF16)],
        grid=(HEADS_LOCAL,),
        flops=8 * 3 * 2 * 512 * 512 * 128,
        nbytes=9 << 20,
        vmem=WIDE,
    )(q, k, v)


def picker(i, copies):
    row = lax.broadcasted_iota(jnp.int32, (8 * copies, HALF), 0) & 7
    lane = lax.broadcasted_iota(jnp.int32, (8 * copies, HALF), 1)
    return jnp.where(row == jnp.where(lane >= 128, 2 * i + 1, 2 * i), 1.0, 0.0).astype(BF16)


def attend_kernel(q_ref, local_ref, g_ref, gain_ref, incoming_ref, first_ref, att_ref, stats_ref, buf, sems):
    copies = []
    for i in range(4):
        tokens = pl.ds(i * HALF, HALF)
        copy = pltpu.make_async_copy(local_ref.at[tokens], buf.at[tokens], sems.at[i])
        copy.start()
        copies.append(copy)
    sums = jnp.zeros((8, HALF), F32)
    for j in (0, 1):
        states = []
        for p in (0, 1):
            rows = pl.ds(p * 256, 256)
            states.append(diagonal(incoming_ref[rows] + first_ref[rows] if j else incoming_ref[rows]))
        for i in (2 * j, 2 * j + 1):
            tokens = pl.ds(i * HALF, HALF)
            square = inner = 0.0
            copies[i].wait()
            for p in (0, 1):
                cols = pl.ds(p * 256, 256)
                att = mm(q_ref[tokens, cols], states[p], NN) + buf[tokens, cols]
                att_ref[tokens, cols] = att
                dot = gain_ref[:, cols] * g_ref[tokens, cols].astype(F32) * att
                att = att * att
                square = square + att[:, :128] + att[:, 128:]
                inner = inner + dot[:, :128] + dot[:, 128:]
            for term in terms(side_by_side(square, inner), 2):
                sums = sums + mm(picker(i, 1), term, NT)
    stats_ref[...] = jnp.broadcast_to(sums[None], stats_ref.shape)


def attend(q, local, g, gain, incoming, first):
    return call(
        attend_kernel,
        [VMEM, ANY] + [VMEM] * 4,
        [VMEM] * 2,
        [struct((1024, 512), F32), struct((8, 8, HALF), F32)],
        scratch=[pltpu.VMEM((1024, 512), F32), pltpu.SemaphoreType.DMA((4,))],
        flops=2 * 1024 * 512 * 128,
        nbytes=6 << 20,
        vmem=LARGE,
    )(q, local, g, gain, incoming, first)


def norm_kernel(att_ref, g_ref, flip_ref, gain_ref, stats_ref, normed_ref, ga_ref, total_ref, last_ref, nbuf, gbuf, lbuf, sems, lsem):
    sums = jnp.concatenate(terms(jnp.sum(stats_ref[...], axis=0), 3), axis=0)
    copies = []
    for j in (0, 1):
        both = pl.ds(j * GROUP, GROUP)
        for i in (2 * j, 2 * j + 1):
            tokens = pl.ds(i * HALF, HALF)
            wide = mm(sums, picker(i, 3), TN)
            inverse = lax.rsqrt(wide[:, :128] * (1.0 / 4096) + EPSILON)
            mean = wide[:, 128:] * inverse * (1.0 / 4096)
            for h in range(HEADS_LOCAL):
                cols = pl.ds(h * HEAD_DIM, HEAD_DIM)
                gain = gain_ref[:, cols]
                unit = att_ref[tokens, cols] * inverse
                nbuf[tokens, cols] = (unit * gain).astype(BF16)
                gbuf[tokens, cols] = ((gain * g_ref[tokens, cols].astype(F32) - unit * mean) * inverse).astype(BF16)
        for n, (buf, out) in enumerate(((nbuf, normed_ref), (gbuf, ga_ref))):
            copy = pltpu.make_async_copy(buf.at[both], out.at[both], sems.at[n, j])
            copy.start()
            copies.append(copy)
        for p in (0, 1):
            pair = pl.ds(p * 256, 256)
            product = mm(flip_ref[pair, both], gbuf[both, pair], NN)
            for n in (0, 1):
                rows = pl.ds(p * 256 + n * 128, 128)
                part = product[n * 128 : n * 128 + 128, n * 128 : n * 128 + 128]
                if j == 0:
                    total_ref[rows] = part
                else:
                    lbuf[rows] = part
                    total_ref[rows] += part
    copy = pltpu.make_async_copy(lbuf, last_ref.at[pl.ds(0, 512)], lsem)
    copy.start()
    copies.append(copy)
    for copy in copies:
        copy.wait()


def norm(att, g, flip, gain, stats):
    return call(
        norm_kernel,
        [VMEM] * 5,
        [ANY, ANY, VMEM, ANY],
        [struct((1024, 512), BF16), struct(BIG_BF16, BF16), struct((512, 128), F32), struct(BIG_LAST, F32)],
        scratch=[pltpu.VMEM((1024, 512), BF16)] * 2
        + [pltpu.VMEM((512, 128), F32), pltpu.SemaphoreType.DMA((2, 2)), pltpu.SemaphoreType.DMA],
        flops=2 * 1024 * 512 * 128,
        nbytes=6 << 20,
        vmem=LARGE,
    )(att, g, flip, gain, stats)


def back_kernel(q_ref, v_ref, ga_ref, early_ref, late_ref, gk_ref, gv_ref):
    upper = triangle(True)
    for j in (0, 1):
        one, two = pl.ds(j * GROUP, HALF), pl.ds(j * GROUP + HALF, HALF)
        both = pl.ds(j * GROUP, GROUP)
        rows = pl.ds(j * HALF, HALF)
        grads = side_by_side(
            jnp.where(upper, mm(v_ref[one], ga_ref[one], NT), 0.0).astype(BF16),
            mm(v_ref[one], ga_ref[two], NT).astype(BF16),
        )
        gk_ref[one] = mm(grads, q_ref[both], NN).astype(BF16)
        grads = jnp.where(upper, mm(v_ref[two], ga_ref[two], NT), 0.0).astype(BF16)
        gk_ref[two] = mm(grads, q_ref[two], NN).astype(BF16)
        gv_ref[one] = mm(early_ref[rows], ga_ref[both], NN).astype(BF16)
        gv_ref[two] = mm(late_ref[rows], ga_ref[two], NN).astype(BF16)


def back(q, v, ga, early, late):
    spec = pl.BlockSpec((2 * GROUP, HEAD_DIM), lambda h: (0, h))
    return call(
        back_kernel,
        [spec] * 3 + [pl.BlockSpec((GROUP, n), lambda h: (h, 0)) for n in (GROUP, HALF)],
        [spec] * 2,
        [struct(BIG_BF16, BF16), struct(BIG_BF16, BF16)],
        grid=(HEADS_LOCAL,),
        flops=8 * 3 * 2 * 512 * 512 * 128,
        nbytes=10 << 20,
        vmem=WIDE,
    )(q, v, ga, early, late)


def query_kernel(k_ref, v_ref, ga_ref, incoming_ref, first_ref, gq_ref):
    lower = triangle(False)
    for j in (0, 1):
        one, two = pl.ds(j * GROUP, HALF), pl.ds(j * GROUP + HALF, HALF)
        both = pl.ds(j * GROUP, GROUP)
        state = (incoming_ref[...] + first_ref[...] if j else incoming_ref[...]).astype(BF16)
        grads = jnp.where(lower, mm(ga_ref[one], v_ref[one], NT), 0.0).astype(BF16)
        gq_ref[one] = (mm(ga_ref[one], state, NT) + mm(grads, k_ref[one], NN)).astype(BF16)
        grads = side_by_side(
            mm(ga_ref[two], v_ref[one], NT).astype(BF16),
            jnp.where(lower, mm(ga_ref[two], v_ref[two], NT), 0.0).astype(BF16),
        )
        gq_ref[two] = (mm(ga_ref[two], state, NT) + mm(grads, k_ref[both], NN)).astype(BF16)


def query_grad(k, v, ga, incoming, first):
    spec = pl.BlockSpec((2 * GROUP, HEAD_DIM), lambda h: (0, h))
    state = pl.BlockSpec((HEAD_DIM, HEAD_DIM), lambda h: (h, 0))
    return call(
        query_kernel,
        [spec] * 3 + [state] * 2,
        spec,
        struct((1024, 512), BF16),
        grid=(HEADS_LOCAL,),
        flops=8 * 2 * 2 * 512 * 512 * 128,
        nbytes=5 << 20,
        vmem=WIDE,
    )(k, v, ga, incoming, first)


def last_kernel(
    k_ref, v_ref, gkl_ref, gvl_ref, arriving_ref, last_hbm, gk_ref, gv_ref, klocal, vlocal, kbuf, vbuf, last_ref, insems, sems, lsem
):
    last_copy = pltpu.make_async_copy(last_hbm.at[pl.ds(0, 512)], last_ref, lsem)
    arrivals = {}
    for j in (1, 0):
        tokens = pl.ds(j * GROUP, GROUP)
        for n, (src, buf) in enumerate(((gkl_ref, klocal), (gvl_ref, vlocal))):
            arrivals[n, j] = pltpu.make_async_copy(src.at[tokens], buf.at[tokens], insems.at[n, j])
            arrivals[n, j].start()
        if j:
            last_copy.start()
    copies = []
    for j in (1, 0):
        tokens = pl.ds(j * GROUP, GROUP)
        suffixes = []
        if not j:
            last_copy.wait()
        for p in (0, 1):
            rows = pl.ds(p * 256, 256)
            suffixes.append(diagonal(arriving_ref[rows] if j else arriving_ref[rows] + last_ref[rows]))
        for n, (x_ref, local, buf, out, dims) in enumerate(
            ((v_ref, klocal, kbuf, gk_ref, NT), (k_ref, vlocal, vbuf, gv_ref, NN))
        ):
            products = [mm(x_ref[tokens, pl.ds(p * 256, 256)], suffixes[p], dims) for p in (0, 1)]
            arrivals[n, j].wait()
            for p in (0, 1):
                cols = pl.ds(p * 256, 256)
                buf[tokens, cols] = (products[p] + local[tokens, cols]).astype(BF16)
            copy = pltpu.make_async_copy(buf.at[tokens], out.at[tokens], sems.at[n, j])
            copy.start()
            copies.append(copy)
    for copy in copies:
        copy.wait()


def finish(k, v, gk_local, gv_local, arriving, last):
    return call(
        last_kernel,
        [VMEM, VMEM, ANY, ANY, VMEM, ANY],
        [ANY] * 2,
        [struct((1024, 512), BF16)] * 2,
        scratch=[pltpu.VMEM((1024, 512), BF16)] * 4
        + [pltpu.VMEM((512, 128), F32)]
        + [pltpu.SemaphoreType.DMA((2, 2))] * 2
        + [pltpu.SemaphoreType.DMA],
        flops=2 * 2 * 1024 * 512 * 128,
        nbytes=8 << 20,
        vmem=LARGE,
    )(k, v, gk_local, gv_local, arriving, last)


def running(pieces, after, reverse):
    def kernel(pieces_ref, after_ref, out_ref):
        run = jnp.zeros(pieces_ref.shape[1:], F32)
        order = range(CTX - 1, -1, -1) if reverse else range(CTX)
        for i in order:
            out_ref[i] = run
            run = run + pieces_ref[i]

    return call(kernel, [VMEM, ANY], VMEM, struct(pieces.shape, F32), flops=1 << 17, nbytes=1 << 19, vmem=LARGE)(
        pieces, after
    )


def exchange(value):
    return lax.all_to_all(value, "ctx", 0, 0, tiled=True)


def split(total):
    return exchange(total.reshape(CTX, 512 // CTX, 128))


def merge(sums):
    return exchange(sums).reshape(512, 128)


def on_device(queries, keys, values, gain, grad_normed):
    gain = gain.reshape(1, 512)
    total, first = moments(keys, values)
    pieces = split(total)
    local, early, late, flip = local_attention(queries, keys, values)
    incoming = merge(running(pieces, local, False))
    att, stats = attend(queries, local, grad_normed, gain, incoming, first)
    stats = lax.all_to_all(stats, "head", 0, 0, tiled=True)
    normed, ga, cototal, last = norm(att, grad_normed, flip, gain, stats)
    pieces = split(cototal)
    gk_local, gv_local = back(queries, values, ga, early, late)
    arriving = merge(running(pieces, gk_local, True))
    gq = query_grad(keys, values, ga, incoming, first)
    gk, gv = finish(keys, values, gk_local, gv_local, arriving, last)
    return normed, gq, gk, gv


def solution(mesh):
    spec = P("ctx", "head")
    return jax.shard_map(
        on_device,
        mesh=mesh,
        in_specs=(spec, spec, spec, P("head"), spec),
        out_specs=(spec,) * 4,
        check_vma=False,
    )
```

```python
import jax
import jax.numpy as jnp
from jax import lax
from jax.experimental import pallas as pl
from jax.experimental.pallas import tpu as pltpu
from jax.sharding import PartitionSpec as P

HEAD_DIM = 128
GROUP = 512
HALF = 256
EPSILON = 1e-06
CTX = 32
HEADS_LOCAL = 4
F32 = jnp.float32
BF16 = jnp.bfloat16


NT = (((1,), (1,)), ((), ()))
TN = (((0,), (0,)), ((), ()))
NN = (((1,), (0,)), ((), ()))


def mm(a, b, dims):
    return lax.dot_general(a, b, dims, preferred_element_type=F32)


def terms(x, count):
    out = []
    for _ in range(count - 1):
        high = x.astype(BF16)
        out.append(high)
        x = x - high.astype(F32)
    return out + [x.astype(BF16)]


def triangle(flip):
    row = lax.broadcasted_iota(jnp.int32, (HALF, HALF), 0)
    col = lax.broadcasted_iota(jnp.int32, (HALF, HALF), 1)
    return (col >= row) if flip else (row >= col)


def diagonal(stacked):
    half = stacked.astype(BF16)
    upper = lax.broadcasted_iota(jnp.int32, half.shape, 0) < HEAD_DIM
    zero = jnp.zeros_like(half)
    return jnp.concatenate([jnp.where(upper, half, zero), jnp.where(upper, zero, half)], axis=1)


def side_by_side(a, b):
    return jnp.concatenate([a, b], axis=1)


WIDE = 60 << 20
LARGE = 44 << 20
BIG_BF16 = (21504, 512)
BIG_F32 = (10752, 512)
BIG_LAST = (43008, 128)


def call(kernel, in_specs, out_specs, out_shape, grid=(), scratch=(), flops=0, nbytes=0, vmem=16 << 20):
    return pl.pallas_call(
        kernel,
        grid=grid,
        in_specs=in_specs,
        out_specs=out_specs,
        out_shape=out_shape,
        scratch_shapes=list(scratch),
        compiler_params=pltpu.CompilerParams(vmem_limit_bytes=vmem),
        cost_estimate=pl.CostEstimate(flops=flops, bytes_accessed=nbytes, transcendentals=0),
    )


VMEM = pl.BlockSpec(memory_space=pltpu.VMEM)
ANY = pl.BlockSpec(memory_space=pl.ANY)


def struct(shape, dtype):
    return jax.ShapeDtypeStruct(shape, dtype)


def moment_kernel(k_hbm, v_hbm, total_ref, k_ref, v_ref, buf, sems, osems):
    copies = []
    for i in range(4):
        tokens = pl.ds(i * HALF, HALF)
        for n, (src, dst) in enumerate(((k_hbm, k_ref), (v_hbm, v_ref))):
            copy = pltpu.make_async_copy(src.at[tokens], dst.at[tokens], sems.at[n, i])
            copy.start()
            copies.append(copy)
    sums = [0.0, 0.0]
    for i in range(4):
        tokens = pl.ds(i * HALF, HALF)
        copies[2 * i].wait()
        copies[2 * i + 1].wait()
        for p in (0, 1):
            cols = pl.ds(p * 256, 256)
            sums[p] = sums[p] + mm(k_ref[tokens, cols], v_ref[tokens, cols], TN)
    copies = []
    for p in (0, 1):
        pair = pl.ds(p * 256, 256)
        buf[pl.ds(p * 256, 128)] = sums[p][:128, :128]
        buf[pl.ds(p * 256 + 128, 128)] = sums[p][128:, 128:]
        copy = pltpu.make_async_copy(buf.at[pair], total_ref.at[pair], osems.at[p])
        copy.start()
        copies.append(copy)
    for copy in copies:
        copy.wait()


def moments(k, v):
    return call(
        moment_kernel,
        [ANY] * 2,
        ANY,
        struct((512, 128), F32),
        scratch=[pltpu.VMEM((1024, 512), BF16)] * 2
        + [pltpu.VMEM((512, 128), F32), pltpu.SemaphoreType.DMA((2, 4)), pltpu.SemaphoreType.DMA((2,))],
        flops=8 * 2 * 512 * 128 * 128,
        nbytes=2 << 20,
        vmem=WIDE,
    )(k, v)


def local_kernel(q_ref, k_ref, v_ref, out_ref, early_ref, late_ref, flip_ref, first_ref):
    first_ref[...] = mm(k_ref[:GROUP], v_ref[:GROUP], TN)
    lower, upper = triangle(False), triangle(True)
    for j in (0, 1):
        one, two = pl.ds(j * GROUP, HALF), pl.ds(j * GROUP + HALF, HALF)
        both = pl.ds(j * GROUP, GROUP)
        probs = jnp.where(lower, mm(q_ref[one], k_ref[one], NT), 0.0).astype(BF16)
        out_ref[one] = mm(probs, v_ref[one], NN)
        probs = side_by_side(
            mm(q_ref[two], k_ref[one], NT).astype(BF16),
            jnp.where(lower, mm(q_ref[two], k_ref[two], NT), 0.0).astype(BF16),
        )
        out_ref[two] = mm(probs, v_ref[both], NN)
        rows = pl.ds(j * HALF, HALF)
        early_ref[rows, :HALF] = jnp.where(upper, mm(k_ref[one], q_ref[one], NT), 0.0).astype(BF16)
        early_ref[rows, HALF:] = mm(k_ref[one], q_ref[two], NT).astype(BF16)
        late_ref[rows] = jnp.where(upper, mm(k_ref[two], q_ref[two], NT), 0.0).astype(BF16)
        flip_ref[:, both] = jnp.transpose(q_ref[both], (1, 0))


def local_attention(q, k, v):
    spec = pl.BlockSpec((2 * GROUP, HEAD_DIM), lambda h: (0, h))
    return call(
        local_kernel,
        [spec] * 3,
        [spec]
        + [pl.BlockSpec((GROUP, n), lambda h: (h, 0)) for n in (GROUP, HALF)]
        + [pl.BlockSpec((HEAD_DIM, n), lambda h: (h, 0)) for n in (1024, HEAD_DIM)],
        [struct(BIG_F32, F32), struct((2048, 512), BF16), struct((2048, 256), BF16), struct((512, 1024), BF16), struct((512, 128), F32)],
        grid=(HEADS_LOCAL,),
        flops=8 * 3 * 2 * 512 * 512 * 128,
        nbytes=9 << 20,
        vmem=WIDE,
    )(q, k, v)


def picker(i, copies):
    row = lax.broadcasted_iota(jnp.int32, (8 * copies, HALF), 0) & 7
    lane = lax.broadcasted_iota(jnp.int32, (8 * copies, HALF), 1)
    return jnp.where(row == jnp.where(lane >= 128, 2 * i + 1, 2 * i), 1.0, 0.0).astype(BF16)


def attend_kernel(q_ref, local_ref, g_ref, gain_ref, incoming_ref, first_ref, att_ref, stats_ref, buf, sems):
    copies = []
    for i in range(4):
        tokens = pl.ds(i * HALF, HALF)
        copy = pltpu.make_async_copy(local_ref.at[tokens], buf.at[tokens], sems.at[i])
        copy.start()
        copies.append(copy)
    sums = jnp.zeros((8, HALF), F32)
    for j in (0, 1):
        states = []
        for p in (0, 1):
            rows = pl.ds(p * 256, 256)
            states.append(diagonal(incoming_ref[rows] + first_ref[rows] if j else incoming_ref[rows]))
        for i in (2 * j, 2 * j + 1):
            tokens = pl.ds(i * HALF, HALF)
            square = inner = 0.0
            products = [mm(q_ref[tokens, pl.ds(p * 256, 256)], states[p], NN) for p in (0, 1)]
            copies[i].wait()
            for p in (0, 1):
                cols = pl.ds(p * 256, 256)
                att = products[p] + buf[tokens, cols]
                att_ref[tokens, cols] = att
                dot = gain_ref[:, cols] * g_ref[tokens, cols].astype(F32) * att
                att = att * att
                square = square + att[:, :128] + att[:, 128:]
                inner = inner + dot[:, :128] + dot[:, 128:]
            for term in terms(side_by_side(square, inner), 2):
                sums = sums + mm(picker(i, 1), term, NT)
    stats_ref[...] = jnp.broadcast_to(sums[None], stats_ref.shape)


def attend(q, local, g, gain, incoming, first):
    return call(
        attend_kernel,
        [VMEM, ANY] + [VMEM] * 4,
        [VMEM] * 2,
        [struct((1024, 512), F32), struct((8, 8, HALF), F32)],
        scratch=[pltpu.VMEM((1024, 512), F32), pltpu.SemaphoreType.DMA((4,))],
        flops=2 * 1024 * 512 * 128,
        nbytes=6 << 20,
        vmem=LARGE,
    )(q, local, g, gain, incoming, first)


def norm_kernel(att_ref, g_ref, flip_ref, gain_ref, stats_ref, normed_ref, ga_ref, total_out, last_ref, nbuf, gbuf, lbuf, total_ref, sems, lsem, tsem):
    sums = jnp.concatenate(terms(jnp.sum(stats_ref[...], axis=0), 3), axis=0)
    copies = []
    for j in (0, 1):
        both = pl.ds(j * GROUP, GROUP)
        for i in (2 * j, 2 * j + 1):
            tokens = pl.ds(i * HALF, HALF)
            wide = mm(sums, picker(i, 3), TN)
            inverse = lax.rsqrt(wide[:, :128] * (1.0 / 4096) + EPSILON)
            mean = wide[:, 128:] * inverse * (1.0 / 4096)
            for h in range(HEADS_LOCAL):
                cols = pl.ds(h * HEAD_DIM, HEAD_DIM)
                gain = gain_ref[:, cols]
                unit = att_ref[tokens, cols] * inverse
                nbuf[tokens, cols] = (unit * gain).astype(BF16)
                gbuf[tokens, cols] = ((gain * g_ref[tokens, cols].astype(F32) - unit * mean) * inverse).astype(BF16)
        for n, (buf, out) in enumerate(((nbuf, normed_ref), (gbuf, ga_ref))):
            copy = pltpu.make_async_copy(buf.at[both], out.at[both], sems.at[n, j])
            copy.start()
            copies.append(copy)
        for p in (0, 1):
            pair = pl.ds(p * 256, 256)
            product = mm(flip_ref[pair, both], gbuf[both, pair], NN)
            for n in (0, 1):
                rows = pl.ds(p * 256 + n * 128, 128)
                part = product[n * 128 : n * 128 + 128, n * 128 : n * 128 + 128]
                if j == 0:
                    total_ref[rows] = part
                else:
                    lbuf[rows] = part
                    total_ref[rows] += part
    for buf, out, sem in ((total_ref, total_out, tsem), (lbuf, last_ref.at[pl.ds(0, 512)], lsem)):
        copy = pltpu.make_async_copy(buf, out, sem)
        copy.start()
        copies.append(copy)
    for copy in copies:
        copy.wait()


def norm(att, g, flip, gain, stats):
    return call(
        norm_kernel,
        [VMEM] * 5,
        [ANY] * 4,
        [struct((1024, 512), BF16), struct(BIG_BF16, BF16), struct((512, 128), F32), struct(BIG_LAST, F32)],
        scratch=[pltpu.VMEM((1024, 512), BF16)] * 2
        + [pltpu.VMEM((512, 128), F32)] * 2
        + [pltpu.SemaphoreType.DMA((2, 2)), pltpu.SemaphoreType.DMA, pltpu.SemaphoreType.DMA],
        flops=2 * 1024 * 512 * 128,
        nbytes=6 << 20,
        vmem=LARGE,
    )(att, g, flip, gain, stats)


def back_kernel(q_ref, v_ref, ga_ref, early_ref, late_ref, gk_ref, gv_ref):
    upper = triangle(True)
    for j in (0, 1):
        one, two = pl.ds(j * GROUP, HALF), pl.ds(j * GROUP + HALF, HALF)
        both = pl.ds(j * GROUP, GROUP)
        rows = pl.ds(j * HALF, HALF)
        grads = side_by_side(
            jnp.where(upper, mm(v_ref[one], ga_ref[one], NT), 0.0).astype(BF16),
            mm(v_ref[one], ga_ref[two], NT).astype(BF16),
        )
        gk_ref[one] = mm(grads, q_ref[both], NN).astype(BF16)
        grads = jnp.where(upper, mm(v_ref[two], ga_ref[two], NT), 0.0).astype(BF16)
        gk_ref[two] = mm(grads, q_ref[two], NN).astype(BF16)
        gv_ref[one] = mm(early_ref[rows], ga_ref[both], NN).astype(BF16)
        gv_ref[two] = mm(late_ref[rows], ga_ref[two], NN).astype(BF16)


def back(q, v, ga, early, late):
    spec = pl.BlockSpec((2 * GROUP, HEAD_DIM), lambda h: (0, h))
    return call(
        back_kernel,
        [spec] * 3 + [pl.BlockSpec((GROUP, n), lambda h: (h, 0)) for n in (GROUP, HALF)],
        [spec] * 2,
        [struct(BIG_BF16, BF16), struct(BIG_BF16, BF16)],
        grid=(HEADS_LOCAL,),
        flops=8 * 3 * 2 * 512 * 512 * 128,
        nbytes=10 << 20,
        vmem=WIDE,
    )(q, v, ga, early, late)


def query_kernel(k_ref, v_ref, ga_ref, incoming_ref, first_ref, gq_ref):
    lower = triangle(False)
    for j in (0, 1):
        one, two = pl.ds(j * GROUP, HALF), pl.ds(j * GROUP + HALF, HALF)
        both = pl.ds(j * GROUP, GROUP)
        state = (incoming_ref[...] + first_ref[...] if j else incoming_ref[...]).astype(BF16)
        grads = jnp.where(lower, mm(ga_ref[one], v_ref[one], NT), 0.0).astype(BF16)
        gq_ref[one] = (mm(ga_ref[one], state, NT) + mm(grads, k_ref[one], NN)).astype(BF16)
        grads = side_by_side(
            mm(ga_ref[two], v_ref[one], NT).astype(BF16),
            jnp.where(lower, mm(ga_ref[two], v_ref[two], NT), 0.0).astype(BF16),
        )
        gq_ref[two] = (mm(ga_ref[two], state, NT) + mm(grads, k_ref[both], NN)).astype(BF16)


def query_grad(k, v, ga, incoming, first):
    spec = pl.BlockSpec((2 * GROUP, HEAD_DIM), lambda h: (0, h))
    state = pl.BlockSpec((HEAD_DIM, HEAD_DIM), lambda h: (h, 0))
    return call(
        query_kernel,
        [spec] * 3 + [state] * 2,
        spec,
        struct((1024, 512), BF16),
        grid=(HEADS_LOCAL,),
        flops=8 * 2 * 2 * 512 * 512 * 128,
        nbytes=5 << 20,
        vmem=WIDE,
    )(k, v, ga, incoming, first)


def last_kernel(
    k_ref, v_ref, gkl_ref, gvl_ref, arriving_ref, last_hbm, gk_ref, gv_ref, klocal, vlocal, kbuf, vbuf, last_ref, insems, sems, lsem
):
    last_copy = pltpu.make_async_copy(last_hbm.at[pl.ds(0, 512)], last_ref, lsem)
    arrivals = {}
    for c in (2, 3, 0, 1):
        tokens = pl.ds(c * HALF, HALF)
        for n, (src, buf) in enumerate(((gkl_ref, klocal), (gvl_ref, vlocal))):
            arrivals[n, c] = pltpu.make_async_copy(src.at[tokens], buf.at[tokens], insems.at[n, c])
            arrivals[n, c].start()
        if c == 3:
            last_copy.start()
    copies = []
    for j in (1, 0):
        suffixes = []
        if not j:
            last_copy.wait()
        for p in (0, 1):
            rows = pl.ds(p * 256, 256)
            suffixes.append(diagonal(arriving_ref[rows] if j else arriving_ref[rows] + last_ref[rows]))
        for c in (2 * j, 2 * j + 1):
            tokens = pl.ds(c * HALF, HALF)
            for n, (x_ref, local, buf, out, dims) in enumerate(
                ((v_ref, klocal, kbuf, gk_ref, NT), (k_ref, vlocal, vbuf, gv_ref, NN))
            ):
                products = [mm(x_ref[tokens, pl.ds(p * 256, 256)], suffixes[p], dims) for p in (0, 1)]
                arrivals[n, c].wait()
                for p in (0, 1):
                    cols = pl.ds(p * 256, 256)
                    buf[tokens, cols] = (products[p] + local[tokens, cols].astype(F32)).astype(BF16)
                copy = pltpu.make_async_copy(buf.at[tokens], out.at[tokens], sems.at[n, c])
                copy.start()
                copies.append(copy)
    for copy in copies:
        copy.wait()


def finish(k, v, gk_local, gv_local, arriving, last):
    return call(
        last_kernel,
        [VMEM, VMEM, ANY, ANY, VMEM, ANY],
        [ANY] * 2,
        [struct((1024, 512), BF16)] * 2,
        scratch=[pltpu.VMEM((1024, 512), BF16)] * 4
        + [pltpu.VMEM((512, 128), F32)]
        + [pltpu.SemaphoreType.DMA((2, 4))] * 2
        + [pltpu.SemaphoreType.DMA],
        flops=2 * 2 * 1024 * 512 * 128,
        nbytes=8 << 20,
        vmem=LARGE,
    )(k, v, gk_local, gv_local, arriving, last)


def running(pieces, after, reverse):
    def kernel(pieces_ref, after_ref, out_ref):
        run = jnp.zeros(pieces_ref.shape[1:], F32)
        order = range(CTX - 1, -1, -1) if reverse else range(CTX)
        for i in order:
            out_ref[i] = run
            run = run + pieces_ref[i]

    return call(kernel, [VMEM, ANY], VMEM, struct(pieces.shape, F32), flops=1 << 17, nbytes=1 << 19, vmem=LARGE)(
        pieces, after
    )


def exchange(value):
    return lax.all_to_all(value, "ctx", 0, 0, tiled=True)


def split(total):
    return exchange(total.reshape(CTX, 512 // CTX, 128))


def merge(sums):
    return exchange(sums).reshape(512, 128)


def on_device(queries, keys, values, gain, grad_normed):
    gain = gain.reshape(1, 512)
    total = moments(keys, values)
    pieces = split(total)
    local, early, late, flip, first = local_attention(queries, keys, values)
    incoming = merge(running(pieces, local, False))
    att, stats = attend(queries, local, grad_normed, gain, incoming, first)
    stats = lax.all_to_all(stats, "head", 0, 0, tiled=True)
    normed, ga, cototal, last = norm(att, grad_normed, flip, gain, stats)
    pieces = split(cototal)
    gk_local, gv_local = back(queries, values, ga, early, late)
    arriving = merge(running(pieces, gk_local, True))
    gq = query_grad(keys, values, ga, incoming, first)
    gk, gv = finish(keys, values, gk_local, gv_local, arriving, last)
    return normed, gq, gk, gv


def solution(mesh):
    spec = P("ctx", "head")
    return jax.shard_map(
        on_device,
        mesh=mesh,
        in_specs=(spec, spec, spec, P("head"), spec),
        out_specs=(spec,) * 4,
        check_vma=False,
    )
```

```python
import jax
import jax.numpy as jnp
from jax import lax
from jax.experimental import pallas as pl
from jax.experimental.pallas import tpu as pltpu
from jax.sharding import PartitionSpec as P

HEAD_DIM = 128
GROUP = 512
HALF = 256
EPSILON = 1e-06
CTX = 32
HEADS_LOCAL = 4
F32 = jnp.float32
BF16 = jnp.bfloat16


NT = (((1,), (1,)), ((), ()))
TN = (((0,), (0,)), ((), ()))
NN = (((1,), (0,)), ((), ()))


def mm(a, b, dims):
    return lax.dot_general(a, b, dims, preferred_element_type=F32)


def terms(x, count):
    out = []
    for _ in range(count - 1):
        high = x.astype(BF16)
        out.append(high)
        x = x - high.astype(F32)
    return out + [x.astype(BF16)]


def triangle(flip):
    row = lax.broadcasted_iota(jnp.int32, (HALF, HALF), 0)
    col = lax.broadcasted_iota(jnp.int32, (HALF, HALF), 1)
    return (col >= row) if flip else (row >= col)


def diagonal(stacked):
    half = stacked.astype(BF16)
    upper = lax.broadcasted_iota(jnp.int32, half.shape, 0) < HEAD_DIM
    zero = jnp.zeros_like(half)
    return jnp.concatenate([jnp.where(upper, half, zero), jnp.where(upper, zero, half)], axis=1)


def side_by_side(a, b):
    return jnp.concatenate([a, b], axis=1)


WIDE = 60 << 20
LARGE = 44 << 20
BIG_BF16 = (21504, 512)
BIG_F32 = (10752, 512)
BIG_LAST = (43008, 128)


def call(kernel, in_specs, out_specs, out_shape, grid=(), scratch=(), flops=0, nbytes=0, vmem=16 << 20):
    return pl.pallas_call(
        kernel,
        grid=grid,
        in_specs=in_specs,
        out_specs=out_specs,
        out_shape=out_shape,
        scratch_shapes=list(scratch),
        compiler_params=pltpu.CompilerParams(vmem_limit_bytes=vmem),
        cost_estimate=pl.CostEstimate(flops=flops, bytes_accessed=nbytes, transcendentals=0),
    )


VMEM = pl.BlockSpec(memory_space=pltpu.VMEM)
ANY = pl.BlockSpec(memory_space=pl.ANY)


def struct(shape, dtype):
    return jax.ShapeDtypeStruct(shape, dtype)


def moment_kernel(k_hbm, v_hbm, total_ref, k_ref, v_ref, buf, sems, osems):
    copies = []
    for i in range(4):
        tokens = pl.ds(i * HALF, HALF)
        for n, (src, dst) in enumerate(((k_hbm, k_ref), (v_hbm, v_ref))):
            copy = pltpu.make_async_copy(src.at[tokens], dst.at[tokens], sems.at[n, i])
            copy.start()
            copies.append(copy)
    sums = [0.0, 0.0]
    for i in range(4):
        tokens = pl.ds(i * HALF, HALF)
        copies[2 * i].wait()
        copies[2 * i + 1].wait()
        for p in (0, 1):
            cols = pl.ds(p * 256, 256)
            sums[p] = sums[p] + mm(k_ref[tokens, cols], v_ref[tokens, cols], TN)
    copies = []
    for p in (0, 1):
        pair = pl.ds(p * 256, 256)
        buf[pl.ds(p * 256, 128)] = sums[p][:128, :128]
        buf[pl.ds(p * 256 + 128, 128)] = sums[p][128:, 128:]
        copy = pltpu.make_async_copy(buf.at[pair], total_ref.at[pair], osems.at[p])
        copy.start()
        copies.append(copy)
    for copy in copies:
        copy.wait()


def moments(k, v):
    return call(
        moment_kernel,
        [ANY] * 2,
        ANY,
        struct((512, 128), F32),
        scratch=[pltpu.VMEM((1024, 512), BF16)] * 2
        + [pltpu.VMEM((512, 128), F32), pltpu.SemaphoreType.DMA((2, 4)), pltpu.SemaphoreType.DMA((2,))],
        flops=8 * 2 * 512 * 128 * 128,
        nbytes=2 << 20,
        vmem=WIDE,
    )(k, v)


def local_kernel(q_ref, k_ref, v_ref, out_ref, early_ref, late_ref, flip_ref, first_ref):
    first_ref[...] = mm(k_ref[:GROUP], v_ref[:GROUP], TN)
    lower, upper = triangle(False), triangle(True)
    for j in (0, 1):
        one, two = pl.ds(j * GROUP, HALF), pl.ds(j * GROUP + HALF, HALF)
        both = pl.ds(j * GROUP, GROUP)
        probs = jnp.where(lower, mm(q_ref[one], k_ref[one], NT), 0.0).astype(BF16)
        out_ref[one] = mm(probs, v_ref[one], NN)
        probs = side_by_side(
            mm(q_ref[two], k_ref[one], NT).astype(BF16),
            jnp.where(lower, mm(q_ref[two], k_ref[two], NT), 0.0).astype(BF16),
        )
        out_ref[two] = mm(probs, v_ref[both], NN)
        rows = pl.ds(j * HALF, HALF)
        early_ref[rows, :HALF] = jnp.where(upper, mm(k_ref[one], q_ref[one], NT), 0.0).astype(BF16)
        early_ref[rows, HALF:] = mm(k_ref[one], q_ref[two], NT).astype(BF16)
        late_ref[rows] = jnp.where(upper, mm(k_ref[two], q_ref[two], NT), 0.0).astype(BF16)
        flip_ref[:, both] = jnp.transpose(q_ref[both], (1, 0))


def local_attention(q, k, v):
    spec = pl.BlockSpec((2 * GROUP, HEAD_DIM), lambda h: (0, h))
    return call(
        local_kernel,
        [spec] * 3,
        [spec]
        + [pl.BlockSpec((GROUP, n), lambda h: (h, 0)) for n in (GROUP, HALF)]
        + [pl.BlockSpec((HEAD_DIM, n), lambda h: (h, 0)) for n in (1024, HEAD_DIM)],
        [struct(BIG_F32, F32), struct((2048, 512), BF16), struct((2048, 256), BF16), struct((512, 1024), BF16), struct((512, 128), F32)],
        grid=(HEADS_LOCAL,),
        flops=8 * 3 * 2 * 512 * 512 * 128,
        nbytes=9 << 20,
        vmem=WIDE,
    )(q, k, v)


def picker(i, copies):
    row = lax.broadcasted_iota(jnp.int32, (8 * copies, HALF), 0) & 7
    lane = lax.broadcasted_iota(jnp.int32, (8 * copies, HALF), 1)
    return jnp.where(row == jnp.where(lane >= 128, 2 * i + 1, 2 * i), 1.0, 0.0).astype(BF16)


def attend_kernel(q_ref, local_ref, g_ref, gain_ref, incoming_ref, first_ref, att_ref, stats_ref, buf, sems):
    copies = []
    for i in range(4):
        tokens = pl.ds(i * HALF, HALF)
        copy = pltpu.make_async_copy(local_ref.at[tokens], buf.at[tokens], sems.at[i])
        copy.start()
        copies.append(copy)
    sums = jnp.zeros((8, HALF), F32)
    for j in (0, 1):
        states = []
        for p in (0, 1):
            rows = pl.ds(p * 256, 256)
            states.append(diagonal(incoming_ref[rows] + first_ref[rows] if j else incoming_ref[rows]))
        both = pl.ds(j * GROUP, GROUP)
        products = [mm(q_ref[both, pl.ds(p * 256, 256)], states[p], NN) for p in (0, 1)]
        for i in (2 * j, 2 * j + 1):
            tokens = pl.ds(i * HALF, HALF)
            square = inner = 0.0
            copies[i].wait()
            part = slice((i - 2 * j) * HALF, (i - 2 * j + 1) * HALF)
            for p in (0, 1):
                cols = pl.ds(p * 256, 256)
                att = products[p][part] + buf[tokens, cols]
                att_ref[tokens, cols] = att
                dot = gain_ref[:, cols] * g_ref[tokens, cols].astype(F32) * att
                att = att * att
                square = square + att[:, :128] + att[:, 128:]
                inner = inner + dot[:, :128] + dot[:, 128:]
            for term in terms(side_by_side(square, inner), 2):
                sums = sums + mm(picker(i, 1), term, NT)
    stats_ref[...] = jnp.broadcast_to(sums[None], stats_ref.shape)


def attend(q, local, g, gain, incoming, first):
    return call(
        attend_kernel,
        [VMEM, ANY] + [VMEM] * 4,
        [VMEM] * 2,
        [struct((1024, 512), F32), struct((8, 8, HALF), F32)],
        scratch=[pltpu.VMEM((1024, 512), F32), pltpu.SemaphoreType.DMA((4,))],
        flops=2 * 1024 * 512 * 128,
        nbytes=6 << 20,
        vmem=LARGE,
    )(q, local, g, gain, incoming, first)


def norm_kernel(att_ref, g_ref, flip_ref, gain_ref, stats_ref, normed_ref, ga_ref, total_out, last_ref, nbuf, gbuf, lbuf, total_ref, sems, lsem, tsem):
    sums = jnp.concatenate(terms(jnp.sum(stats_ref[...], axis=0), 3), axis=0)
    copies = []
    for j in (0, 1):
        both = pl.ds(j * GROUP, GROUP)
        for i in (2 * j, 2 * j + 1):
            tokens = pl.ds(i * HALF, HALF)
            wide = mm(sums, picker(i, 3), TN)
            inverse = lax.rsqrt(wide[:, :128] * (1.0 / 4096) + EPSILON)
            mean = wide[:, 128:] * inverse * (1.0 / 4096)
            for h in range(HEADS_LOCAL):
                cols = pl.ds(h * HEAD_DIM, HEAD_DIM)
                gain = gain_ref[:, cols]
                unit = att_ref[tokens, cols] * inverse
                nbuf[tokens, cols] = (unit * gain).astype(BF16)
                gbuf[tokens, cols] = ((gain * g_ref[tokens, cols].astype(F32) - unit * mean) * inverse).astype(BF16)
        for n, (buf, out) in enumerate(((nbuf, normed_ref), (gbuf, ga_ref))):
            copy = pltpu.make_async_copy(buf.at[both], out.at[both], sems.at[n, j])
            copy.start()
            copies.append(copy)
        for p in (0, 1):
            pair = pl.ds(p * 256, 256)
            product = mm(flip_ref[pair, both], gbuf[both, pair], NN)
            for n in (0, 1):
                rows = pl.ds(p * 256 + n * 128, 128)
                part = product[n * 128 : n * 128 + 128, n * 128 : n * 128 + 128]
                if j == 0:
                    total_ref[rows] = part
                else:
                    lbuf[rows] = part
                    total_ref[rows] += part
    for buf, out, sem in ((total_ref, total_out, tsem), (lbuf, last_ref.at[pl.ds(0, 512)], lsem)):
        copy = pltpu.make_async_copy(buf, out, sem)
        copy.start()
        copies.append(copy)
    for copy in copies:
        copy.wait()


def norm(att, g, flip, gain, stats):
    return call(
        norm_kernel,
        [VMEM] * 5,
        [ANY] * 4,
        [struct((1024, 512), BF16), struct(BIG_BF16, BF16), struct((512, 128), F32), struct(BIG_LAST, F32)],
        scratch=[pltpu.VMEM((1024, 512), BF16)] * 2
        + [pltpu.VMEM((512, 128), F32)] * 2
        + [pltpu.SemaphoreType.DMA((2, 2)), pltpu.SemaphoreType.DMA, pltpu.SemaphoreType.DMA],
        flops=2 * 1024 * 512 * 128,
        nbytes=6 << 20,
        vmem=LARGE,
    )(att, g, flip, gain, stats)


def back_kernel(q_ref, v_ref, ga_ref, early_ref, late_ref, gk_ref, gv_ref):
    upper = triangle(True)
    for j in (0, 1):
        one, two = pl.ds(j * GROUP, HALF), pl.ds(j * GROUP + HALF, HALF)
        both = pl.ds(j * GROUP, GROUP)
        rows = pl.ds(j * HALF, HALF)
        grads = side_by_side(
            jnp.where(upper, mm(v_ref[one], ga_ref[one], NT), 0.0).astype(BF16),
            mm(v_ref[one], ga_ref[two], NT).astype(BF16),
        )
        gk_ref[one] = mm(grads, q_ref[both], NN).astype(BF16)
        grads = jnp.where(upper, mm(v_ref[two], ga_ref[two], NT), 0.0).astype(BF16)
        gk_ref[two] = mm(grads, q_ref[two], NN).astype(BF16)
        gv_ref[one] = mm(early_ref[rows], ga_ref[both], NN).astype(BF16)
        gv_ref[two] = mm(late_ref[rows], ga_ref[two], NN).astype(BF16)


def back(q, v, ga, early, late):
    spec = pl.BlockSpec((2 * GROUP, HEAD_DIM), lambda h: (0, h))
    return call(
        back_kernel,
        [spec] * 3 + [pl.BlockSpec((GROUP, n), lambda h: (h, 0)) for n in (GROUP, HALF)],
        [spec] * 2,
        [struct(BIG_BF16, BF16), struct(BIG_BF16, BF16)],
        grid=(HEADS_LOCAL,),
        flops=8 * 3 * 2 * 512 * 512 * 128,
        nbytes=10 << 20,
        vmem=WIDE,
    )(q, v, ga, early, late)


def query_kernel(k_ref, v_ref, ga_ref, incoming_ref, first_ref, gq_ref):
    lower = triangle(False)
    for j in (0, 1):
        one, two = pl.ds(j * GROUP, HALF), pl.ds(j * GROUP + HALF, HALF)
        both = pl.ds(j * GROUP, GROUP)
        state = (incoming_ref[...] + first_ref[...] if j else incoming_ref[...]).astype(BF16)
        grads = jnp.where(lower, mm(ga_ref[one], v_ref[one], NT), 0.0).astype(BF16)
        gq_ref[one] = (mm(ga_ref[one], state, NT) + mm(grads, k_ref[one], NN)).astype(BF16)
        grads = side_by_side(
            mm(ga_ref[two], v_ref[one], NT).astype(BF16),
            jnp.where(lower, mm(ga_ref[two], v_ref[two], NT), 0.0).astype(BF16),
        )
        gq_ref[two] = (mm(ga_ref[two], state, NT) + mm(grads, k_ref[both], NN)).astype(BF16)


def query_grad(k, v, ga, incoming, first):
    spec = pl.BlockSpec((2 * GROUP, HEAD_DIM), lambda h: (0, h))
    state = pl.BlockSpec((HEAD_DIM, HEAD_DIM), lambda h: (h, 0))
    return call(
        query_kernel,
        [spec] * 3 + [state] * 2,
        spec,
        struct((1024, 512), BF16),
        grid=(HEADS_LOCAL,),
        flops=8 * 2 * 2 * 512 * 512 * 128,
        nbytes=5 << 20,
        vmem=WIDE,
    )(k, v, ga, incoming, first)


def last_kernel(
    k_ref, v_ref, gkl_ref, gvl_ref, arriving_ref, last_hbm, gk_ref, gv_ref, klocal, vlocal, kbuf, vbuf, last_ref, insems, sems, lsem
):
    last_copy = pltpu.make_async_copy(last_hbm.at[pl.ds(0, 512)], last_ref, lsem)
    arrivals = {}
    for c in (2, 3, 0, 1):
        tokens = pl.ds(c * HALF, HALF)
        for n, (src, buf) in enumerate(((gkl_ref, klocal), (gvl_ref, vlocal))):
            arrivals[n, c] = pltpu.make_async_copy(src.at[tokens], buf.at[tokens], insems.at[n, c])
            arrivals[n, c].start()
        if c == 3:
            last_copy.start()
    copies = []
    for j in (1, 0):
        suffixes = []
        if not j:
            last_copy.wait()
        for p in (0, 1):
            rows = pl.ds(p * 256, 256)
            suffixes.append(diagonal(arriving_ref[rows] if j else arriving_ref[rows] + last_ref[rows]))
        both = pl.ds(j * GROUP, GROUP)
        for n, (x_ref, local, buf, out, dims) in enumerate(
            ((v_ref, klocal, kbuf, gk_ref, NT), (k_ref, vlocal, vbuf, gv_ref, NN))
        ):
            products = [mm(x_ref[both, pl.ds(p * 256, 256)], suffixes[p], dims) for p in (0, 1)]
            for c in (0, 1):
                i = 2 * j + c
                tokens = pl.ds(i * HALF, HALF)
                arrivals[n, i].wait()
                for p in (0, 1):
                    cols = pl.ds(p * 256, 256)
                    product = products[p][c * HALF : c * HALF + HALF]
                    buf[tokens, cols] = (product + local[tokens, cols].astype(F32)).astype(BF16)
                copy = pltpu.make_async_copy(buf.at[tokens], out.at[tokens], sems.at[n, i])
                copy.start()
                copies.append(copy)
    for copy in copies:
        copy.wait()


def finish(k, v, gk_local, gv_local, arriving, last):
    return call(
        last_kernel,
        [VMEM, VMEM, ANY, ANY, VMEM, ANY],
        [ANY] * 2,
        [struct((1024, 512), BF16)] * 2,
        scratch=[pltpu.VMEM((1024, 512), BF16)] * 4
        + [pltpu.VMEM((512, 128), F32)]
        + [pltpu.SemaphoreType.DMA((2, 4))] * 2
        + [pltpu.SemaphoreType.DMA],
        flops=2 * 2 * 1024 * 512 * 128,
        nbytes=8 << 20,
        vmem=LARGE,
    )(k, v, gk_local, gv_local, arriving, last)


def running(pieces, after, reverse):
    def kernel(pieces_ref, after_ref, out_ref):
        run = jnp.zeros(pieces_ref.shape[1:], F32)
        order = range(CTX - 1, -1, -1) if reverse else range(CTX)
        for i in order:
            out_ref[i] = run
            run = run + pieces_ref[i]

    return call(kernel, [VMEM, ANY], VMEM, struct(pieces.shape, F32), flops=1 << 17, nbytes=1 << 19, vmem=LARGE)(
        pieces, after
    )


def exchange(value):
    return lax.all_to_all(value, "ctx", 0, 0, tiled=True)


def split(total):
    return exchange(total.reshape(CTX, 512 // CTX, 128))


def merge(sums):
    return exchange(sums).reshape(512, 128)


def on_device(queries, keys, values, gain, grad_normed):
    gain = gain.reshape(1, 512)
    total = moments(keys, values)
    pieces = split(total)
    local, early, late, flip, first = local_attention(queries, keys, values)
    incoming = merge(running(pieces, local, False))
    att, stats = attend(queries, local, grad_normed, gain, incoming, first)
    stats = lax.all_to_all(stats, "head", 0, 0, tiled=True)
    normed, ga, cototal, last = norm(att, grad_normed, flip, gain, stats)
    pieces = split(cototal)
    gk_local, gv_local = back(queries, values, ga, early, late)
    arriving = merge(running(pieces, gk_local, True))
    gq = query_grad(keys, values, ga, incoming, first)
    gk, gv = finish(keys, values, gk_local, gv_local, arriving, last)
    return normed, gq, gk, gv


def solution(mesh):
    spec = P("ctx", "head")
    return jax.shard_map(
        on_device,
        mesh=mesh,
        in_specs=(spec, spec, spec, P("head"), spec),
        out_specs=(spec,) * 4,
        check_vma=False,
    )
```

```python
import jax
import jax.numpy as jnp
from jax import lax
from jax.experimental import pallas as pl
from jax.experimental.pallas import tpu as pltpu
from jax.sharding import PartitionSpec as P

HEAD_DIM = 128
GROUP = 512
HALF = 256
EPSILON = 1e-06
CTX = 32
HEADS_LOCAL = 4
F32 = jnp.float32
BF16 = jnp.bfloat16


NT = (((1,), (1,)), ((), ()))
TN = (((0,), (0,)), ((), ()))
NN = (((1,), (0,)), ((), ()))


def mm(a, b, dims):
    return lax.dot_general(a, b, dims, preferred_element_type=F32)


def terms(x, count):
    out = []
    for _ in range(count - 1):
        high = x.astype(BF16)
        out.append(high)
        x = x - high.astype(F32)
    return out + [x.astype(BF16)]


def triangle(flip):
    row = lax.broadcasted_iota(jnp.int32, (HALF, HALF), 0)
    col = lax.broadcasted_iota(jnp.int32, (HALF, HALF), 1)
    return (col >= row) if flip else (row >= col)


def diagonal(stacked):
    half = stacked.astype(BF16)
    upper = lax.broadcasted_iota(jnp.int32, half.shape, 0) < HEAD_DIM
    zero = jnp.zeros_like(half)
    return jnp.concatenate([jnp.where(upper, half, zero), jnp.where(upper, zero, half)], axis=1)


def side_by_side(a, b):
    return jnp.concatenate([a, b], axis=1)


WIDE = 60 << 20
LARGE = 44 << 20
BIG_BF16 = (21504, 512)
BIG_F32 = (10752, 512)
BIG_LAST = (43008, 128)


def call(kernel, in_specs, out_specs, out_shape, grid=(), scratch=(), flops=0, nbytes=0, vmem=16 << 20):
    return pl.pallas_call(
        kernel,
        grid=grid,
        in_specs=in_specs,
        out_specs=out_specs,
        out_shape=out_shape,
        scratch_shapes=list(scratch),
        compiler_params=pltpu.CompilerParams(vmem_limit_bytes=vmem),
        cost_estimate=pl.CostEstimate(flops=flops, bytes_accessed=nbytes, transcendentals=0),
    )


VMEM = pl.BlockSpec(memory_space=pltpu.VMEM)
ANY = pl.BlockSpec(memory_space=pl.ANY)


def struct(shape, dtype):
    return jax.ShapeDtypeStruct(shape, dtype)


def moment_kernel(k_hbm, v_hbm, total_ref, k_ref, v_ref, buf, sems, osems):
    copies = []
    for i in range(4):
        tokens = pl.ds(i * HALF, HALF)
        for n, (src, dst) in enumerate(((k_hbm, k_ref), (v_hbm, v_ref))):
            copy = pltpu.make_async_copy(src.at[tokens], dst.at[tokens], sems.at[n, i])
            copy.start()
            copies.append(copy)
    sums = [0.0, 0.0]
    for i in range(4):
        tokens = pl.ds(i * HALF, HALF)
        copies[2 * i].wait()
        copies[2 * i + 1].wait()
        for p in (0, 1):
            cols = pl.ds(p * 256, 256)
            sums[p] = sums[p] + mm(k_ref[tokens, cols], v_ref[tokens, cols], TN)
    copies = []
    for p in (0, 1):
        pair = pl.ds(p * 256, 256)
        buf[pl.ds(p * 256, 128)] = sums[p][:128, :128]
        buf[pl.ds(p * 256 + 128, 128)] = sums[p][128:, 128:]
        copy = pltpu.make_async_copy(buf.at[pair], total_ref.at[pair], osems.at[p])
        copy.start()
        copies.append(copy)
    for copy in copies:
        copy.wait()


def moments(k, v):
    return call(
        moment_kernel,
        [ANY] * 2,
        ANY,
        struct((512, 128), F32),
        scratch=[pltpu.VMEM((1024, 512), BF16)] * 2
        + [pltpu.VMEM((512, 128), F32), pltpu.SemaphoreType.DMA((2, 4)), pltpu.SemaphoreType.DMA((2,))],
        flops=8 * 2 * 512 * 128 * 128,
        nbytes=2 << 20,
        vmem=WIDE,
    )(k, v)


def local_kernel(q_ref, k_ref, v_ref, out_ref, early_ref, late_ref, flip_ref, first_ref):
    first_ref[...] = mm(k_ref[:GROUP], v_ref[:GROUP], TN)
    lower, upper = triangle(False), triangle(True)
    for j in (0, 1):
        one, two = pl.ds(j * GROUP, HALF), pl.ds(j * GROUP + HALF, HALF)
        both = pl.ds(j * GROUP, GROUP)
        probs = jnp.where(lower, mm(q_ref[one], k_ref[one], NT), 0.0).astype(BF16)
        out_ref[one] = mm(probs, v_ref[one], NN)
        probs = side_by_side(
            mm(q_ref[two], k_ref[one], NT).astype(BF16),
            jnp.where(lower, mm(q_ref[two], k_ref[two], NT), 0.0).astype(BF16),
        )
        out_ref[two] = mm(probs, v_ref[both], NN)
        rows = pl.ds(j * HALF, HALF)
        early_ref[rows, :HALF] = jnp.where(upper, mm(k_ref[one], q_ref[one], NT), 0.0).astype(BF16)
        early_ref[rows, HALF:] = mm(k_ref[one], q_ref[two], NT).astype(BF16)
        late_ref[rows] = jnp.where(upper, mm(k_ref[two], q_ref[two], NT), 0.0).astype(BF16)
        flip_ref[:, both] = jnp.transpose(q_ref[both], (1, 0))


def local_attention(q, k, v):
    spec = pl.BlockSpec((2 * GROUP, HEAD_DIM), lambda h: (0, h))
    return call(
        local_kernel,
        [spec] * 3,
        [spec]
        + [pl.BlockSpec((GROUP, n), lambda h: (h, 0)) for n in (GROUP, HALF)]
        + [pl.BlockSpec((HEAD_DIM, n), lambda h: (h, 0)) for n in (1024, HEAD_DIM)],
        [struct(BIG_F32, F32), struct((2048, 512), BF16), struct((2048, 256), BF16), struct((512, 1024), BF16), struct((512, 128), F32)],
        grid=(HEADS_LOCAL,),
        flops=8 * 3 * 2 * 512 * 512 * 128,
        nbytes=9 << 20,
        vmem=WIDE,
    )(q, k, v)


def picker(i, copies):
    row = lax.broadcasted_iota(jnp.int32, (8 * copies, HALF), 0) & 7
    lane = lax.broadcasted_iota(jnp.int32, (8 * copies, HALF), 1)
    return jnp.where(row == jnp.where(lane >= 128, 2 * i + 1, 2 * i), 1.0, 0.0).astype(BF16)


def attend_kernel(q_ref, local_ref, g_ref, gain_ref, incoming_ref, first_ref, att_ref, stats_ref, buf, sems):
    copies = []
    for i in range(4):
        tokens = pl.ds(i * HALF, HALF)
        copy = pltpu.make_async_copy(local_ref.at[tokens], buf.at[tokens], sems.at[i])
        copy.start()
        copies.append(copy)
    sums = jnp.zeros((8, HALF), F32)
    for j in (0, 1):
        states = []
        for p in (0, 1):
            rows = pl.ds(p * 256, 256)
            states.append(diagonal(incoming_ref[rows] + first_ref[rows] if j else incoming_ref[rows]))
        both = pl.ds(j * GROUP, GROUP)
        products = [mm(q_ref[both, pl.ds(p * 256, 256)], states[p], NN) for p in (0, 1)]
        for i in (2 * j, 2 * j + 1):
            tokens = pl.ds(i * HALF, HALF)
            square = inner = 0.0
            copies[i].wait()
            part = slice((i - 2 * j) * HALF, (i - 2 * j + 1) * HALF)
            for p in (0, 1):
                cols = pl.ds(p * 256, 256)
                att = products[p][part] + buf[tokens, cols]
                att_ref[tokens, cols] = att
                dot = gain_ref[:, cols] * g_ref[tokens, cols].astype(F32) * att
                att = att * att
                square = square + att[:, :128] + att[:, 128:]
                inner = inner + dot[:, :128] + dot[:, 128:]
            for term in terms(side_by_side(square, inner), 2):
                sums = sums + mm(picker(i, 1), term, NT)
    stats_ref[...] = jnp.broadcast_to(sums[None], stats_ref.shape)


def attend(q, local, g, gain, incoming, first):
    return call(
        attend_kernel,
        [VMEM, ANY] + [VMEM] * 4,
        [VMEM] * 2,
        [struct((1024, 512), F32), struct((8, 8, HALF), F32)],
        scratch=[pltpu.VMEM((1024, 512), F32), pltpu.SemaphoreType.DMA((4,))],
        flops=2 * 1024 * 512 * 128,
        nbytes=6 << 20,
        vmem=LARGE,
    )(q, local, g, gain, incoming, first)


def norm_kernel(att_ref, g_ref, flip_ref, gain_ref, stats_ref, normed_ref, ga_ref, total_out, last_ref, nbuf, gbuf, lbuf, total_ref, sems, lsem, tsem):
    sums = jnp.concatenate(terms(jnp.sum(stats_ref[...], axis=0), 3), axis=0)
    copies = []
    for j in (0, 1):
        both = pl.ds(j * GROUP, GROUP)
        for i in (2 * j, 2 * j + 1):
            tokens = pl.ds(i * HALF, HALF)
            wide = mm(sums, picker(i, 3), TN)
            inverse = lax.rsqrt(wide[:, :128] * (1.0 / 4096) + EPSILON)
            mean = wide[:, 128:] * inverse * (1.0 / 4096)
            for h in range(HEADS_LOCAL):
                cols = pl.ds(h * HEAD_DIM, HEAD_DIM)
                gain = gain_ref[:, cols]
                unit = att_ref[tokens, cols] * inverse
                nbuf[tokens, cols] = (unit * gain).astype(BF16)
                gbuf[tokens, cols] = ((gain * g_ref[tokens, cols].astype(F32) - unit * mean) * inverse).astype(BF16)
        for n, (buf, out) in enumerate(((nbuf, normed_ref), (gbuf, ga_ref))):
            copy = pltpu.make_async_copy(buf.at[both], out.at[both], sems.at[n, j])
            copy.start()
            copies.append(copy)
        for p in (0, 1):
            pair = pl.ds(p * 256, 256)
            product = mm(flip_ref[pair, both], gbuf[both, pair], NN)
            for n in (0, 1):
                rows = pl.ds(p * 256 + n * 128, 128)
                part = product[n * 128 : n * 128 + 128, n * 128 : n * 128 + 128]
                if j == 0:
                    total_ref[rows] = part
                else:
                    lbuf[rows] = part
                    total_ref[rows] += part
    for buf, out, sem in ((total_ref, total_out, tsem), (lbuf, last_ref.at[pl.ds(0, 512)], lsem)):
        copy = pltpu.make_async_copy(buf, out, sem)
        copy.start()
        copies.append(copy)
    for copy in copies:
        copy.wait()


def norm(att, g, flip, gain, stats):
    return call(
        norm_kernel,
        [VMEM] * 5,
        [ANY] * 4,
        [struct((1024, 512), BF16), struct(BIG_BF16, BF16), struct((512, 128), F32), struct(BIG_LAST, F32)],
        scratch=[pltpu.VMEM((1024, 512), BF16)] * 2
        + [pltpu.VMEM((512, 128), F32)] * 2
        + [pltpu.SemaphoreType.DMA((2, 2)), pltpu.SemaphoreType.DMA, pltpu.SemaphoreType.DMA],
        flops=2 * 1024 * 512 * 128,
        nbytes=6 << 20,
        vmem=LARGE,
    )(att, g, flip, gain, stats)


def back_kernel(q_ref, v_ref, ga_ref, early_ref, late_ref, gk_ref, gv_ref):
    upper = triangle(True)
    for j in (0, 1):
        one, two = pl.ds(j * GROUP, HALF), pl.ds(j * GROUP + HALF, HALF)
        both = pl.ds(j * GROUP, GROUP)
        rows = pl.ds(j * HALF, HALF)
        grads = side_by_side(
            jnp.where(upper, mm(v_ref[one], ga_ref[one], NT), 0.0).astype(BF16),
            mm(v_ref[one], ga_ref[two], NT).astype(BF16),
        )
        gk_ref[one] = mm(grads, q_ref[both], NN).astype(BF16)
        grads = jnp.where(upper, mm(v_ref[two], ga_ref[two], NT), 0.0).astype(BF16)
        gk_ref[two] = mm(grads, q_ref[two], NN).astype(BF16)
        gv_ref[one] = mm(early_ref[rows], ga_ref[both], NN).astype(BF16)
        gv_ref[two] = mm(late_ref[rows], ga_ref[two], NN).astype(BF16)


def back(q, v, ga, early, late):
    spec = pl.BlockSpec((2 * GROUP, HEAD_DIM), lambda h: (0, h))
    return call(
        back_kernel,
        [spec] * 3 + [pl.BlockSpec((GROUP, n), lambda h: (h, 0)) for n in (GROUP, HALF)],
        [spec] * 2,
        [struct(BIG_BF16, BF16), struct(BIG_BF16, BF16)],
        grid=(HEADS_LOCAL,),
        flops=8 * 3 * 2 * 512 * 512 * 128,
        nbytes=10 << 20,
        vmem=WIDE,
    )(q, v, ga, early, late)


def query_kernel(k_ref, v_ref, ga_ref, incoming_ref, first_ref, gq_ref):
    lower = triangle(False)
    for j in (0, 1):
        one, two = pl.ds(j * GROUP, HALF), pl.ds(j * GROUP + HALF, HALF)
        both = pl.ds(j * GROUP, GROUP)
        state = (incoming_ref[...] + first_ref[...] if j else incoming_ref[...]).astype(BF16)
        grads = jnp.where(lower, mm(ga_ref[one], v_ref[one], NT), 0.0).astype(BF16)
        gq_ref[one] = (mm(ga_ref[one], state, NT) + mm(grads, k_ref[one], NN)).astype(BF16)
        grads = side_by_side(
            mm(ga_ref[two], v_ref[one], NT).astype(BF16),
            jnp.where(lower, mm(ga_ref[two], v_ref[two], NT), 0.0).astype(BF16),
        )
        gq_ref[two] = (mm(ga_ref[two], state, NT) + mm(grads, k_ref[both], NN)).astype(BF16)


def query_grad(k, v, ga, incoming, first):
    spec = pl.BlockSpec((2 * GROUP, HEAD_DIM), lambda h: (0, h))
    state = pl.BlockSpec((HEAD_DIM, HEAD_DIM), lambda h: (h, 0))
    return call(
        query_kernel,
        [spec] * 3 + [state] * 2,
        spec,
        struct((1024, 512), BF16),
        grid=(HEADS_LOCAL,),
        flops=8 * 2 * 2 * 512 * 512 * 128,
        nbytes=5 << 20,
        vmem=WIDE,
    )(k, v, ga, incoming, first)


def last_kernel(
    k_ref, v_ref, gkl_ref, gvl_ref, arriving_ref, last_hbm, gk_ref, gv_ref, klocal, vlocal, kbuf, vbuf, last_ref, insems, sems, lsem
):
    last_copy = pltpu.make_async_copy(last_hbm.at[pl.ds(0, 512)], last_ref, lsem)
    arrivals = {}
    for c in (2, 3, 0, 1):
        tokens = pl.ds(c * HALF, HALF)
        for n, (src, buf) in enumerate(((gkl_ref, klocal), (gvl_ref, vlocal))):
            arrivals[n, c] = pltpu.make_async_copy(src.at[tokens], buf.at[tokens], insems.at[n, c])
            arrivals[n, c].start()
        if c == 3:
            last_copy.start()
    copies = []
    for j in (1, 0):
        suffixes = []
        if not j:
            last_copy.wait()
        for p in (0, 1):
            rows = pl.ds(p * 256, 256)
            suffixes.append(diagonal(arriving_ref[rows] if j else arriving_ref[rows] + last_ref[rows]))
        both = pl.ds(j * GROUP, GROUP)
        products = [
            [mm(x_ref[both, pl.ds(p * 256, 256)], suffixes[p], dims) for p in (0, 1)]
            for x_ref, dims in ((v_ref, NT), (k_ref, NN))
        ]
        for n, (local, buf, out) in enumerate(((klocal, kbuf, gk_ref), (vlocal, vbuf, gv_ref))):
            for c in (0, 1):
                i = 2 * j + c
                tokens = pl.ds(i * HALF, HALF)
                arrivals[n, i].wait()
                for p in (0, 1):
                    cols = pl.ds(p * 256, 256)
                    product = products[n][p][c * HALF : c * HALF + HALF]
                    buf[tokens, cols] = (product + local[tokens, cols].astype(F32)).astype(BF16)
                copy = pltpu.make_async_copy(buf.at[tokens], out.at[tokens], sems.at[n, i])
                copy.start()
                copies.append(copy)
    for copy in copies:
        copy.wait()


def finish(k, v, gk_local, gv_local, arriving, last):
    return call(
        last_kernel,
        [VMEM, VMEM, ANY, ANY, VMEM, ANY],
        [ANY] * 2,
        [struct((1024, 512), BF16)] * 2,
        scratch=[pltpu.VMEM((1024, 512), BF16)] * 4
        + [pltpu.VMEM((512, 128), F32)]
        + [pltpu.SemaphoreType.DMA((2, 4))] * 2
        + [pltpu.SemaphoreType.DMA],
        flops=2 * 2 * 1024 * 512 * 128,
        nbytes=8 << 20,
        vmem=LARGE,
    )(k, v, gk_local, gv_local, arriving, last)


def running(pieces, after, reverse):
    def kernel(pieces_ref, after_ref, out_ref):
        run = jnp.zeros(pieces_ref.shape[1:], F32)
        order = range(CTX - 1, -1, -1) if reverse else range(CTX)
        for i in order:
            out_ref[i] = run
            run = run + pieces_ref[i]

    return call(kernel, [VMEM, ANY], VMEM, struct(pieces.shape, F32), flops=1 << 17, nbytes=1 << 19, vmem=LARGE)(
        pieces, after
    )


def exchange(value):
    return lax.all_to_all(value, "ctx", 0, 0, tiled=True)


def split(total):
    return exchange(total.reshape(CTX, 512 // CTX, 128))


def merge(sums):
    return exchange(sums).reshape(512, 128)


def on_device(queries, keys, values, gain, grad_normed):
    gain = gain.reshape(1, 512)
    total = moments(keys, values)
    pieces = split(total)
    local, early, late, flip, first = local_attention(queries, keys, values)
    incoming = merge(running(pieces, local, False))
    att, stats = attend(queries, local, grad_normed, gain, incoming, first)
    stats = lax.all_to_all(stats, "head", 0, 0, tiled=True)
    normed, ga, cototal, last = norm(att, grad_normed, flip, gain, stats)
    pieces = split(cototal)
    gk_local, gv_local = back(queries, values, ga, early, late)
    arriving = merge(running(pieces, gk_local, True))
    gq = query_grad(keys, values, ga, incoming, first)
    gk, gv = finish(keys, values, gk_local, gv_local, arriving, last)
    return normed, gq, gk, gv


def solution(mesh):
    spec = P("ctx", "head")
    return jax.shard_map(
        on_device,
        mesh=mesh,
        in_specs=(spec, spec, spec, P("head"), spec),
        out_specs=(spec,) * 4,
        check_vma=False,
    )
```

```python
import jax
import jax.numpy as jnp
from jax import lax
from jax.experimental import pallas as pl
from jax.experimental.pallas import tpu as pltpu
from jax.sharding import PartitionSpec as P

HEAD_DIM = 128
GROUP = 512
HALF = 256
EPSILON = 1e-06
CTX = 32
HEADS_LOCAL = 4
F32 = jnp.float32
BF16 = jnp.bfloat16


NT = (((1,), (1,)), ((), ()))
TN = (((0,), (0,)), ((), ()))
NN = (((1,), (0,)), ((), ()))


def mm(a, b, dims):
    return lax.dot_general(a, b, dims, preferred_element_type=F32)


def terms(x, count):
    out = []
    for _ in range(count - 1):
        high = x.astype(BF16)
        out.append(high)
        x = x - high.astype(F32)
    return out + [x.astype(BF16)]


def triangle(flip):
    row = lax.broadcasted_iota(jnp.int32, (HALF, HALF), 0)
    col = lax.broadcasted_iota(jnp.int32, (HALF, HALF), 1)
    return (col >= row) if flip else (row >= col)


def diagonal(stacked):
    half = stacked.astype(BF16)
    upper = lax.broadcasted_iota(jnp.int32, half.shape, 0) < HEAD_DIM
    zero = jnp.zeros_like(half)
    return jnp.concatenate([jnp.where(upper, half, zero), jnp.where(upper, zero, half)], axis=1)


def side_by_side(a, b):
    return jnp.concatenate([a, b], axis=1)


WIDE = 60 << 20
LARGE = 44 << 20
BIG_BF16 = (21504, 512)
BIG_F32 = (10752, 512)
BIG_LAST = (43008, 128)


def call(kernel, in_specs, out_specs, out_shape, grid=(), scratch=(), flops=0, nbytes=0, vmem=16 << 20):
    return pl.pallas_call(
        kernel,
        grid=grid,
        in_specs=in_specs,
        out_specs=out_specs,
        out_shape=out_shape,
        scratch_shapes=list(scratch),
        compiler_params=pltpu.CompilerParams(vmem_limit_bytes=vmem),
        cost_estimate=pl.CostEstimate(flops=flops, bytes_accessed=nbytes, transcendentals=0),
    )


VMEM = pl.BlockSpec(memory_space=pltpu.VMEM)
ANY = pl.BlockSpec(memory_space=pl.ANY)


def struct(shape, dtype):
    return jax.ShapeDtypeStruct(shape, dtype)


def moment_kernel(k_hbm, v_hbm, total_ref, k_ref, v_ref, buf, sems, osems):
    copies = []
    for i in range(4):
        tokens = pl.ds(i * HALF, HALF)
        for n, (src, dst) in enumerate(((k_hbm, k_ref), (v_hbm, v_ref))):
            copy = pltpu.make_async_copy(src.at[tokens], dst.at[tokens], sems.at[n, i])
            copy.start()
            copies.append(copy)
    sums = [0.0, 0.0]
    for i in range(4):
        tokens = pl.ds(i * HALF, HALF)
        copies[2 * i].wait()
        copies[2 * i + 1].wait()
        for p in (0, 1):
            cols = pl.ds(p * 256, 256)
            sums[p] = sums[p] + mm(k_ref[tokens, cols], v_ref[tokens, cols], TN)
    copies = []
    for p in (0, 1):
        pair = pl.ds(p * 256, 256)
        buf[pl.ds(p * 256, 128)] = sums[p][:128, :128]
        buf[pl.ds(p * 256 + 128, 128)] = sums[p][128:, 128:]
        copy = pltpu.make_async_copy(buf.at[pair], total_ref.at[pair], osems.at[p])
        copy.start()
        copies.append(copy)
    for copy in copies:
        copy.wait()


def moments(k, v):
    return call(
        moment_kernel,
        [ANY] * 2,
        ANY,
        struct((512, 128), F32),
        scratch=[pltpu.VMEM((1024, 512), BF16)] * 2
        + [pltpu.VMEM((512, 128), F32), pltpu.SemaphoreType.DMA((2, 4)), pltpu.SemaphoreType.DMA((2,))],
        flops=8 * 2 * 512 * 128 * 128,
        nbytes=2 << 20,
        vmem=WIDE,
    )(k, v)


def local_kernel(q_ref, k_ref, v_ref, out_ref, early_ref, late_ref, flip_ref, first_ref):
    first_ref[...] = mm(k_ref[:GROUP], v_ref[:GROUP], TN)
    lower, upper = triangle(False), triangle(True)
    for j in (0, 1):
        one, two = pl.ds(j * GROUP, HALF), pl.ds(j * GROUP + HALF, HALF)
        both = pl.ds(j * GROUP, GROUP)
        probs = jnp.where(lower, mm(q_ref[one], k_ref[one], NT), 0.0).astype(BF16)
        out_ref[one] = mm(probs, v_ref[one], NN)
        probs = side_by_side(
            mm(q_ref[two], k_ref[one], NT).astype(BF16),
            jnp.where(lower, mm(q_ref[two], k_ref[two], NT), 0.0).astype(BF16),
        )
        out_ref[two] = mm(probs, v_ref[both], NN)
        rows = pl.ds(j * HALF, HALF)
        early_ref[rows, :HALF] = jnp.where(upper, mm(k_ref[one], q_ref[one], NT), 0.0).astype(BF16)
        early_ref[rows, HALF:] = mm(k_ref[one], q_ref[two], NT).astype(BF16)
        late_ref[rows] = jnp.where(upper, mm(k_ref[two], q_ref[two], NT), 0.0).astype(BF16)
        flip_ref[:, both] = jnp.transpose(q_ref[both], (1, 0))


def local_attention(q, k, v):
    spec = pl.BlockSpec((2 * GROUP, HEAD_DIM), lambda h: (0, h))
    return call(
        local_kernel,
        [spec] * 3,
        [spec]
        + [pl.BlockSpec((GROUP, n), lambda h: (h, 0)) for n in (GROUP, HALF)]
        + [pl.BlockSpec((HEAD_DIM, n), lambda h: (h, 0)) for n in (1024, HEAD_DIM)],
        [struct(BIG_F32, F32), struct((2048, 512), BF16), struct((2048, 256), BF16), struct((512, 1024), BF16), struct((512, 128), F32)],
        grid=(HEADS_LOCAL,),
        flops=8 * 3 * 2 * 512 * 512 * 128,
        nbytes=9 << 20,
        vmem=WIDE,
    )(q, k, v)


def picker(i, copies):
    row = lax.broadcasted_iota(jnp.int32, (8 * copies, HALF), 0) & 7
    lane = lax.broadcasted_iota(jnp.int32, (8 * copies, HALF), 1)
    return jnp.where(row == jnp.where(lane >= 128, 2 * i + 1, 2 * i), 1.0, 0.0).astype(BF16)


def attend_kernel(q_ref, local_ref, g_ref, gain_ref, incoming_ref, first_ref, att_ref, stats_ref, buf, sems):
    copies = []
    for i in range(4):
        tokens = pl.ds(i * HALF, HALF)
        copy = pltpu.make_async_copy(local_ref.at[tokens], buf.at[tokens], sems.at[i])
        copy.start()
        copies.append(copy)
    sums = jnp.zeros((8, HALF), F32)
    for j in (0, 1):
        states = []
        for p in (0, 1):
            rows = pl.ds(p * 256, 256)
            states.append(diagonal(incoming_ref[rows] + first_ref[rows] if j else incoming_ref[rows]))
        both = pl.ds(j * GROUP, GROUP)
        products = [mm(q_ref[both, pl.ds(p * 256, 256)], states[p], NN) for p in (0, 1)]
        for i in (2 * j, 2 * j + 1):
            tokens = pl.ds(i * HALF, HALF)
            square = inner = 0.0
            copies[i].wait()
            part = slice((i - 2 * j) * HALF, (i - 2 * j + 1) * HALF)
            for p in (0, 1):
                cols = pl.ds(p * 256, 256)
                att = products[p][part] + buf[tokens, cols]
                att_ref[tokens, cols] = att
                dot = gain_ref[:, cols] * g_ref[tokens, cols].astype(F32) * att
                att = att * att
                square = square + att[:, :128] + att[:, 128:]
                inner = inner + dot[:, :128] + dot[:, 128:]
            for term in terms(side_by_side(square, inner), 2):
                sums = sums + mm(picker(i, 1), term, NT)
    stats_ref[...] = jnp.broadcast_to(sums[None], stats_ref.shape)


def attend(q, local, g, gain, incoming, first):
    return call(
        attend_kernel,
        [VMEM, ANY] + [VMEM] * 4,
        [VMEM] * 2,
        [struct((1024, 512), F32), struct((8, 8, HALF), F32)],
        scratch=[pltpu.VMEM((1024, 512), F32), pltpu.SemaphoreType.DMA((4,))],
        flops=2 * 1024 * 512 * 128,
        nbytes=6 << 20,
        vmem=LARGE,
    )(q, local, g, gain, incoming, first)


def norm_kernel(att_ref, g_ref, flip_ref, gain_ref, stats_ref, normed_ref, ga_ref, total_out, last_ref, nbuf, gbuf, lbuf, total_ref, sems, lsem, tsem):
    sums = jnp.concatenate(terms(jnp.sum(stats_ref[...], axis=0), 3), axis=0)
    copies = []
    for j in (0, 1):
        both = pl.ds(j * GROUP, GROUP)
        for i in (2 * j, 2 * j + 1):
            tokens = pl.ds(i * HALF, HALF)
            wide = mm(sums, picker(i, 3), TN)
            inverse = lax.rsqrt(wide[:, :128] * (1.0 / 4096) + EPSILON)
            mean = wide[:, 128:] * inverse * (1.0 / 4096)
            for h in range(HEADS_LOCAL):
                cols = pl.ds(h * HEAD_DIM, HEAD_DIM)
                gain = gain_ref[:, cols]
                unit = att_ref[tokens, cols] * inverse
                nbuf[tokens, cols] = (unit * gain).astype(BF16)
                gbuf[tokens, cols] = ((gain * g_ref[tokens, cols].astype(F32) - unit * mean) * inverse).astype(BF16)
        for n, (buf, out) in enumerate(((nbuf, normed_ref), (gbuf, ga_ref))):
            copy = pltpu.make_async_copy(buf.at[both], out.at[both], sems.at[n, j])
            copy.start()
            copies.append(copy)
        for p in (0, 1):
            pair = pl.ds(p * 256, 256)
            product = mm(flip_ref[pair, both], gbuf[both, pair], NN)
            for n in (0, 1):
                rows = pl.ds(p * 256 + n * 128, 128)
                part = product[n * 128 : n * 128 + 128, n * 128 : n * 128 + 128]
                if j == 0:
                    total_ref[rows] = part
                else:
                    lbuf[rows] = part
                    total_ref[rows] += part
    for buf, out, sem in ((total_ref, total_out, tsem), (lbuf, last_ref.at[pl.ds(0, 512)], lsem)):
        copy = pltpu.make_async_copy(buf, out, sem)
        copy.start()
        copies.append(copy)
    for copy in copies:
        copy.wait()


def norm(att, g, flip, gain, stats):
    return call(
        norm_kernel,
        [VMEM] * 5,
        [ANY] * 4,
        [struct((1024, 512), BF16), struct(BIG_BF16, BF16), struct((512, 128), F32), struct(BIG_LAST, F32)],
        scratch=[pltpu.VMEM((1024, 512), BF16)] * 2
        + [pltpu.VMEM((512, 128), F32)] * 2
        + [pltpu.SemaphoreType.DMA((2, 2)), pltpu.SemaphoreType.DMA, pltpu.SemaphoreType.DMA],
        flops=2 * 1024 * 512 * 128,
        nbytes=6 << 20,
        vmem=LARGE,
    )(att, g, flip, gain, stats)


def back_kernel(q_ref, v_ref, ga_ref, early_ref, late_ref, gk_ref, gv_ref):
    upper = triangle(True)
    for j in (0, 1):
        one, two = pl.ds(j * GROUP, HALF), pl.ds(j * GROUP + HALF, HALF)
        both = pl.ds(j * GROUP, GROUP)
        rows = pl.ds(j * HALF, HALF)
        grads = side_by_side(
            jnp.where(upper, mm(v_ref[one], ga_ref[one], NT), 0.0).astype(BF16),
            mm(v_ref[one], ga_ref[two], NT).astype(BF16),
        )
        gk_ref[one] = mm(grads, q_ref[both], NN).astype(BF16)
        grads = jnp.where(upper, mm(v_ref[two], ga_ref[two], NT), 0.0).astype(BF16)
        gk_ref[two] = mm(grads, q_ref[two], NN).astype(BF16)
        gv_ref[one] = mm(early_ref[rows], ga_ref[both], NN).astype(BF16)
        gv_ref[two] = mm(late_ref[rows], ga_ref[two], NN).astype(BF16)


def back(q, v, ga, early, late):
    spec = pl.BlockSpec((2 * GROUP, HEAD_DIM), lambda h: (0, h))
    return call(
        back_kernel,
        [spec] * 3 + [pl.BlockSpec((GROUP, n), lambda h: (h, 0)) for n in (GROUP, HALF)],
        [spec] * 2,
        [struct((1024, 512), BF16), struct(BIG_BF16, BF16)],
        grid=(HEADS_LOCAL,),
        flops=8 * 3 * 2 * 512 * 512 * 128,
        nbytes=10 << 20,
        vmem=WIDE,
    )(q, v, ga, early, late)


def query_kernel(k_ref, v_ref, ga_ref, incoming_ref, first_ref, gq_ref):
    lower = triangle(False)
    for j in (0, 1):
        one, two = pl.ds(j * GROUP, HALF), pl.ds(j * GROUP + HALF, HALF)
        both = pl.ds(j * GROUP, GROUP)
        state = (incoming_ref[...] + first_ref[...] if j else incoming_ref[...]).astype(BF16)
        grads = jnp.where(lower, mm(ga_ref[one], v_ref[one], NT), 0.0).astype(BF16)
        gq_ref[one] = (mm(ga_ref[one], state, NT) + mm(grads, k_ref[one], NN)).astype(BF16)
        grads = side_by_side(
            mm(ga_ref[two], v_ref[one], NT).astype(BF16),
            jnp.where(lower, mm(ga_ref[two], v_ref[two], NT), 0.0).astype(BF16),
        )
        gq_ref[two] = (mm(ga_ref[two], state, NT) + mm(grads, k_ref[both], NN)).astype(BF16)


def query_grad(k, v, ga, incoming, first):
    spec = pl.BlockSpec((2 * GROUP, HEAD_DIM), lambda h: (0, h))
    state = pl.BlockSpec((HEAD_DIM, HEAD_DIM), lambda h: (h, 0))
    return call(
        query_kernel,
        [spec] * 3 + [state] * 2,
        spec,
        struct((1024, 512), BF16),
        grid=(HEADS_LOCAL,),
        flops=8 * 2 * 2 * 512 * 512 * 128,
        nbytes=5 << 20,
        vmem=WIDE,
    )(k, v, ga, incoming, first)


def last_kernel(
    k_ref, v_ref, gkl_ref, gvl_ref, arriving_ref, last_hbm, gk_ref, gv_ref, vlocal, kbuf, vbuf, last_ref, insems, sems, lsem
):
    last_copy = pltpu.make_async_copy(last_hbm.at[pl.ds(0, 512)], last_ref, lsem)
    arrivals = {}
    for c in (2, 3, 0, 1):
        tokens = pl.ds(c * HALF, HALF)
        arrivals[c] = pltpu.make_async_copy(gvl_ref.at[tokens], vlocal.at[tokens], insems.at[c])
        arrivals[c].start()
        if c == 3:
            last_copy.start()
    copies = []
    for j in (1, 0):
        suffixes = []
        if not j:
            last_copy.wait()
        for p in (0, 1):
            rows = pl.ds(p * 256, 256)
            suffixes.append(diagonal(arriving_ref[rows] if j else arriving_ref[rows] + last_ref[rows]))
        both = pl.ds(j * GROUP, GROUP)
        products = [
            [mm(x_ref[both, pl.ds(p * 256, 256)], suffixes[p], dims) for p in (0, 1)]
            for x_ref, dims in ((v_ref, NT), (k_ref, NN))
        ]
        for n, (local, buf, out) in enumerate(((gkl_ref, kbuf, gk_ref), (vlocal, vbuf, gv_ref))):
            for c in (0, 1):
                i = 2 * j + c
                tokens = pl.ds(i * HALF, HALF)
                if n:
                    arrivals[i].wait()
                for p in (0, 1):
                    cols = pl.ds(p * 256, 256)
                    product = products[n][p][c * HALF : c * HALF + HALF]
                    buf[tokens, cols] = (product + local[tokens, cols].astype(F32)).astype(BF16)
                copy = pltpu.make_async_copy(buf.at[tokens], out.at[tokens], sems.at[n, i])
                copy.start()
                copies.append(copy)
    for copy in copies:
        copy.wait()


def finish(k, v, gk_local, gv_local, arriving, last):
    return call(
        last_kernel,
        [VMEM, VMEM, VMEM, ANY, VMEM, ANY],
        [ANY] * 2,
        [struct((1024, 512), BF16)] * 2,
        scratch=[pltpu.VMEM((1024, 512), BF16)] * 3
        + [pltpu.VMEM((512, 128), F32)]
        + [pltpu.SemaphoreType.DMA((4,)), pltpu.SemaphoreType.DMA((2, 4)), pltpu.SemaphoreType.DMA],
        flops=2 * 2 * 1024 * 512 * 128,
        nbytes=8 << 20,
        vmem=LARGE,
    )(k, v, gk_local, gv_local, arriving, last)


def running(pieces, after, reverse):
    def kernel(pieces_ref, after_ref, out_ref):
        run = jnp.zeros(pieces_ref.shape[1:], F32)
        order = range(CTX - 1, -1, -1) if reverse else range(CTX)
        for i in order:
            out_ref[i] = run
            run = run + pieces_ref[i]

    return call(kernel, [VMEM, ANY], VMEM, struct(pieces.shape, F32), flops=1 << 17, nbytes=1 << 19, vmem=LARGE)(
        pieces, after
    )


def exchange(value):
    return lax.all_to_all(value, "ctx", 0, 0, tiled=True)


def split(total):
    return exchange(total.reshape(CTX, 512 // CTX, 128))


def merge(sums):
    return exchange(sums).reshape(512, 128)


def on_device(queries, keys, values, gain, grad_normed):
    gain = gain.reshape(1, 512)
    total = moments(keys, values)
    pieces = split(total)
    local, early, late, flip, first = local_attention(queries, keys, values)
    incoming = merge(running(pieces, local, False))
    att, stats = attend(queries, local, grad_normed, gain, incoming, first)
    stats = lax.all_to_all(stats, "head", 0, 0, tiled=True)
    normed, ga, cototal, last = norm(att, grad_normed, flip, gain, stats)
    pieces = split(cototal)
    gk_local, gv_local = back(queries, values, ga, early, late)
    arriving = merge(running(pieces, gv_local, True))
    gq = query_grad(keys, values, ga, incoming, first)
    gk, gv = finish(keys, values, gk_local, gv_local, arriving, last)
    return normed, gq, gk, gv


def solution(mesh):
    spec = P("ctx", "head")
    return jax.shard_map(
        on_device,
        mesh=mesh,
        in_specs=(spec, spec, spec, P("head"), spec),
        out_specs=(spec,) * 4,
        check_vma=False,
    )
```

```python
import jax
import jax.numpy as jnp
from jax import lax
from jax.experimental import pallas as pl
from jax.experimental.pallas import tpu as pltpu
from jax.sharding import PartitionSpec as P

HEAD_DIM = 128
GROUP = 512
HALF = 256
EPSILON = 1e-06
CTX = 32
HEADS_LOCAL = 4
F32 = jnp.float32
BF16 = jnp.bfloat16


NT = (((1,), (1,)), ((), ()))
TN = (((0,), (0,)), ((), ()))
NN = (((1,), (0,)), ((), ()))


def mm(a, b, dims):
    return lax.dot_general(a, b, dims, preferred_element_type=F32)


def terms(x, count):
    out = []
    for _ in range(count - 1):
        high = x.astype(BF16)
        out.append(high)
        x = x - high.astype(F32)
    return out + [x.astype(BF16)]


def triangle(flip):
    row = lax.broadcasted_iota(jnp.int32, (HALF, HALF), 0)
    col = lax.broadcasted_iota(jnp.int32, (HALF, HALF), 1)
    return (col >= row) if flip else (row >= col)


def diagonal(stacked):
    half = stacked.astype(BF16)
    upper = lax.broadcasted_iota(jnp.int32, half.shape, 0) < HEAD_DIM
    zero = jnp.zeros_like(half)
    return jnp.concatenate([jnp.where(upper, half, zero), jnp.where(upper, zero, half)], axis=1)


def side_by_side(a, b):
    return jnp.concatenate([a, b], axis=1)


WIDE = 60 << 20
LARGE = 44 << 20
BIG_BF16 = (21504, 512)
BIG_F32 = (10752, 512)
BIG_LAST = (43008, 128)


def call(kernel, in_specs, out_specs, out_shape, grid=(), scratch=(), flops=0, nbytes=0, vmem=16 << 20):
    return pl.pallas_call(
        kernel,
        grid=grid,
        in_specs=in_specs,
        out_specs=out_specs,
        out_shape=out_shape,
        scratch_shapes=list(scratch),
        compiler_params=pltpu.CompilerParams(vmem_limit_bytes=vmem),
        cost_estimate=pl.CostEstimate(flops=flops, bytes_accessed=nbytes, transcendentals=0),
    )


VMEM = pl.BlockSpec(memory_space=pltpu.VMEM)
ANY = pl.BlockSpec(memory_space=pl.ANY)


def struct(shape, dtype):
    return jax.ShapeDtypeStruct(shape, dtype)


def moment_kernel(k_hbm, v_hbm, total_ref, k_ref, v_ref, buf, sems, osems):
    copies = []
    for i in range(4):
        tokens = pl.ds(i * HALF, HALF)
        for n, (src, dst) in enumerate(((k_hbm, k_ref), (v_hbm, v_ref))):
            copy = pltpu.make_async_copy(src.at[tokens], dst.at[tokens], sems.at[n, i])
            copy.start()
            copies.append(copy)
    sums = [0.0, 0.0]
    for i in range(4):
        tokens = pl.ds(i * HALF, HALF)
        copies[2 * i].wait()
        copies[2 * i + 1].wait()
        for p in (0, 1):
            cols = pl.ds(p * 256, 256)
            sums[p] = sums[p] + mm(k_ref[tokens, cols], v_ref[tokens, cols], TN)
    copies = []
    for p in (0, 1):
        pair = pl.ds(p * 256, 256)
        buf[pl.ds(p * 256, 128)] = sums[p][:128, :128]
        buf[pl.ds(p * 256 + 128, 128)] = sums[p][128:, 128:]
        copy = pltpu.make_async_copy(buf.at[pair], total_ref.at[pair], osems.at[p])
        copy.start()
        copies.append(copy)
    for copy in copies:
        copy.wait()


def moments(k, v):
    return call(
        moment_kernel,
        [ANY] * 2,
        ANY,
        struct((512, 128), F32),
        scratch=[pltpu.VMEM((1024, 512), BF16)] * 2
        + [pltpu.VMEM((512, 128), F32), pltpu.SemaphoreType.DMA((2, 4)), pltpu.SemaphoreType.DMA((2,))],
        flops=8 * 2 * 512 * 128 * 128,
        nbytes=2 << 20,
        vmem=WIDE,
    )(k, v)


def local_kernel(q_ref, k_ref, v_ref, out_ref, early_ref, late_ref, flip_ref, first_ref):
    first_ref[...] = mm(k_ref[:GROUP], v_ref[:GROUP], TN)
    lower, upper = triangle(False), triangle(True)
    for j in (0, 1):
        one, two = pl.ds(j * GROUP, HALF), pl.ds(j * GROUP + HALF, HALF)
        both = pl.ds(j * GROUP, GROUP)
        probs = jnp.where(lower, mm(q_ref[one], k_ref[one], NT), 0.0).astype(BF16)
        out_ref[one] = mm(probs, v_ref[one], NN)
        probs = side_by_side(
            mm(q_ref[two], k_ref[one], NT).astype(BF16),
            jnp.where(lower, mm(q_ref[two], k_ref[two], NT), 0.0).astype(BF16),
        )
        out_ref[two] = mm(probs, v_ref[both], NN)
        rows = pl.ds(j * HALF, HALF)
        early_ref[rows, :HALF] = jnp.where(upper, mm(k_ref[one], q_ref[one], NT), 0.0).astype(BF16)
        early_ref[rows, HALF:] = mm(k_ref[one], q_ref[two], NT).astype(BF16)
        late_ref[rows] = jnp.where(upper, mm(k_ref[two], q_ref[two], NT), 0.0).astype(BF16)
        flip_ref[:, both] = jnp.transpose(q_ref[both], (1, 0))


def local_attention(q, k, v):
    spec = pl.BlockSpec((2 * GROUP, HEAD_DIM), lambda h: (0, h))
    return call(
        local_kernel,
        [spec] * 3,
        [spec]
        + [pl.BlockSpec((GROUP, n), lambda h: (h, 0)) for n in (GROUP, HALF)]
        + [pl.BlockSpec((HEAD_DIM, n), lambda h: (h, 0)) for n in (1024, HEAD_DIM)],
        [struct(BIG_F32, F32), struct((2048, 512), BF16), struct((2048, 256), BF16), struct((512, 1024), BF16), struct((512, 128), F32)],
        grid=(HEADS_LOCAL,),
        flops=8 * 3 * 2 * 512 * 512 * 128,
        nbytes=9 << 20,
        vmem=WIDE,
    )(q, k, v)


def picker(i, copies):
    row = lax.broadcasted_iota(jnp.int32, (8 * copies, HALF), 0) & 7
    lane = lax.broadcasted_iota(jnp.int32, (8 * copies, HALF), 1)
    return jnp.where(row == jnp.where(lane >= 128, 2 * i + 1, 2 * i), 1.0, 0.0).astype(BF16)


def attend_kernel(q_ref, local_ref, g_ref, gain_ref, incoming_ref, first_ref, att_ref, stats_ref, buf, sems):
    copies = []
    for i in range(4):
        tokens = pl.ds(i * HALF, HALF)
        copy = pltpu.make_async_copy(local_ref.at[tokens], buf.at[tokens], sems.at[i])
        copy.start()
        copies.append(copy)
    sums = jnp.zeros((8, HALF), F32)
    for j in (0, 1):
        states = []
        for p in (0, 1):
            rows = pl.ds(p * 256, 256)
            states.append(diagonal(incoming_ref[rows] + first_ref[rows] if j else incoming_ref[rows]))
        both = pl.ds(j * GROUP, GROUP)
        products = [mm(q_ref[both, pl.ds(p * 256, 256)], states[p], NN) for p in (0, 1)]
        for i in (2 * j, 2 * j + 1):
            tokens = pl.ds(i * HALF, HALF)
            square = inner = 0.0
            copies[i].wait()
            part = slice((i - 2 * j) * HALF, (i - 2 * j + 1) * HALF)
            for p in (0, 1):
                cols = pl.ds(p * 256, 256)
                att = products[p][part] + buf[tokens, cols]
                att_ref[tokens, cols] = att
                dot = gain_ref[:, cols] * g_ref[tokens, cols].astype(F32) * att
                att = att * att
                square = square + att[:, :128] + att[:, 128:]
                inner = inner + dot[:, :128] + dot[:, 128:]
            for term in terms(side_by_side(square, inner), 2):
                sums = sums + mm(picker(i, 1), term, NT)
    stats_ref[...] = jnp.broadcast_to(sums[None], stats_ref.shape)


def attend(q, local, g, gain, incoming, first):
    return call(
        attend_kernel,
        [VMEM, ANY] + [VMEM] * 4,
        [VMEM] * 2,
        [struct((1024, 512), F32), struct((8, 8, HALF), F32)],
        scratch=[pltpu.VMEM((1024, 512), F32), pltpu.SemaphoreType.DMA((4,))],
        flops=2 * 1024 * 512 * 128,
        nbytes=6 << 20,
        vmem=LARGE,
    )(q, local, g, gain, incoming, first)


def norm_kernel(att_ref, g_ref, flip_ref, gain_ref, stats_ref, normed_ref, ga_ref, total_out, last_ref, nbuf, gbuf, lbuf, total_ref, sems, lsem, tsem):
    sums = jnp.concatenate(terms(jnp.sum(stats_ref[...], axis=0), 3), axis=0)
    copies = []
    for j in (0, 1):
        both = pl.ds(j * GROUP, GROUP)
        for i in (2 * j, 2 * j + 1):
            tokens = pl.ds(i * HALF, HALF)
            wide = mm(sums, picker(i, 3), TN)
            inverse = lax.rsqrt(wide[:, :128] * (1.0 / 4096) + EPSILON)
            mean = wide[:, 128:] * inverse * (1.0 / 4096)
            for h in range(HEADS_LOCAL):
                cols = pl.ds(h * HEAD_DIM, HEAD_DIM)
                gain = gain_ref[:, cols]
                unit = att_ref[tokens, cols] * inverse
                nbuf[tokens, cols] = (unit * gain).astype(BF16)
                gbuf[tokens, cols] = ((gain * g_ref[tokens, cols].astype(F32) - unit * mean) * inverse).astype(BF16)
            for n, (buf, out) in enumerate(((nbuf, normed_ref), (gbuf, ga_ref))):
                copy = pltpu.make_async_copy(buf.at[tokens], out.at[tokens], sems.at[n, i])
                copy.start()
                copies.append(copy)
        for p in (0, 1):
            pair = pl.ds(p * 256, 256)
            product = mm(flip_ref[pair, both], gbuf[both, pair], NN)
            for n in (0, 1):
                rows = pl.ds(p * 256 + n * 128, 128)
                part = product[n * 128 : n * 128 + 128, n * 128 : n * 128 + 128]
                if j == 0:
                    total_ref[rows] = part
                else:
                    lbuf[rows] = part
                    total_ref[rows] += part
    for buf, out, sem in ((total_ref, total_out, tsem), (lbuf, last_ref.at[pl.ds(0, 512)], lsem)):
        copy = pltpu.make_async_copy(buf, out, sem)
        copy.start()
        copies.append(copy)
    for copy in copies:
        copy.wait()


def norm(att, g, flip, gain, stats):
    return call(
        norm_kernel,
        [VMEM] * 5,
        [ANY] * 4,
        [struct((1024, 512), BF16), struct(BIG_BF16, BF16), struct((512, 128), F32), struct(BIG_LAST, F32)],
        scratch=[pltpu.VMEM((1024, 512), BF16)] * 2
        + [pltpu.VMEM((512, 128), F32)] * 2
        + [pltpu.SemaphoreType.DMA((2, 4)), pltpu.SemaphoreType.DMA, pltpu.SemaphoreType.DMA],
        flops=2 * 1024 * 512 * 128,
        nbytes=6 << 20,
        vmem=LARGE,
    )(att, g, flip, gain, stats)


def back_kernel(q_ref, v_ref, ga_ref, early_ref, late_ref, gk_ref, gv_ref):
    upper = triangle(True)
    for j in (0, 1):
        one, two = pl.ds(j * GROUP, HALF), pl.ds(j * GROUP + HALF, HALF)
        both = pl.ds(j * GROUP, GROUP)
        rows = pl.ds(j * HALF, HALF)
        grads = side_by_side(
            jnp.where(upper, mm(v_ref[one], ga_ref[one], NT), 0.0).astype(BF16),
            mm(v_ref[one], ga_ref[two], NT).astype(BF16),
        )
        gk_ref[one] = mm(grads, q_ref[both], NN).astype(BF16)
        grads = jnp.where(upper, mm(v_ref[two], ga_ref[two], NT), 0.0).astype(BF16)
        gk_ref[two] = mm(grads, q_ref[two], NN).astype(BF16)
        gv_ref[one] = mm(early_ref[rows], ga_ref[both], NN).astype(BF16)
        gv_ref[two] = mm(late_ref[rows], ga_ref[two], NN).astype(BF16)


def back(q, v, ga, early, late):
    spec = pl.BlockSpec((2 * GROUP, HEAD_DIM), lambda h: (0, h))
    return call(
        back_kernel,
        [spec] * 3 + [pl.BlockSpec((GROUP, n), lambda h: (h, 0)) for n in (GROUP, HALF)],
        [spec] * 2,
        [struct((1024, 512), BF16), struct(BIG_BF16, BF16)],
        grid=(HEADS_LOCAL,),
        flops=8 * 3 * 2 * 512 * 512 * 128,
        nbytes=10 << 20,
        vmem=WIDE,
    )(q, v, ga, early, late)


def query_kernel(k_ref, v_ref, ga_ref, incoming_ref, first_ref, gq_ref):
    lower = triangle(False)
    for j in (0, 1):
        one, two = pl.ds(j * GROUP, HALF), pl.ds(j * GROUP + HALF, HALF)
        both = pl.ds(j * GROUP, GROUP)
        state = (incoming_ref[...] + first_ref[...] if j else incoming_ref[...]).astype(BF16)
        grads = jnp.where(lower, mm(ga_ref[one], v_ref[one], NT), 0.0).astype(BF16)
        gq_ref[one] = (mm(ga_ref[one], state, NT) + mm(grads, k_ref[one], NN)).astype(BF16)
        grads = side_by_side(
            mm(ga_ref[two], v_ref[one], NT).astype(BF16),
            jnp.where(lower, mm(ga_ref[two], v_ref[two], NT), 0.0).astype(BF16),
        )
        gq_ref[two] = (mm(ga_ref[two], state, NT) + mm(grads, k_ref[both], NN)).astype(BF16)


def query_grad(k, v, ga, incoming, first):
    spec = pl.BlockSpec((2 * GROUP, HEAD_DIM), lambda h: (0, h))
    state = pl.BlockSpec((HEAD_DIM, HEAD_DIM), lambda h: (h, 0))
    return call(
        query_kernel,
        [spec] * 3 + [state] * 2,
        spec,
        struct((1024, 512), BF16),
        grid=(HEADS_LOCAL,),
        flops=8 * 2 * 2 * 512 * 512 * 128,
        nbytes=5 << 20,
        vmem=WIDE,
    )(k, v, ga, incoming, first)


def last_kernel(
    k_ref, v_ref, gkl_ref, gvl_ref, arriving_ref, last_hbm, gk_ref, gv_ref, vlocal, kbuf, vbuf, last_ref, insems, sems, lsem
):
    last_copy = pltpu.make_async_copy(last_hbm.at[pl.ds(0, 512)], last_ref, lsem)
    arrivals = {}
    for c in (2, 3, 0, 1):
        tokens = pl.ds(c * HALF, HALF)
        arrivals[c] = pltpu.make_async_copy(gvl_ref.at[tokens], vlocal.at[tokens], insems.at[c])
        arrivals[c].start()
        if c == 3:
            last_copy.start()
    copies = []
    for j in (1, 0):
        suffixes = []
        if not j:
            last_copy.wait()
        for p in (0, 1):
            rows = pl.ds(p * 256, 256)
            suffixes.append(diagonal(arriving_ref[rows] if j else arriving_ref[rows] + last_ref[rows]))
        both = pl.ds(j * GROUP, GROUP)
        products = [
            [mm(x_ref[both, pl.ds(p * 256, 256)], suffixes[p], dims) for p in (0, 1)]
            for x_ref, dims in ((v_ref, NT), (k_ref, NN))
        ]
        for n, (local, buf, out) in enumerate(((gkl_ref, kbuf, gk_ref), (vlocal, vbuf, gv_ref))):
            for c in (0, 1):
                i = 2 * j + c
                tokens = pl.ds(i * HALF, HALF)
                if n:
                    arrivals[i].wait()
                for p in (0, 1):
                    cols = pl.ds(p * 256, 256)
                    product = products[n][p][c * HALF : c * HALF + HALF]
                    buf[tokens, cols] = (product + local[tokens, cols].astype(F32)).astype(BF16)
                copy = pltpu.make_async_copy(buf.at[tokens], out.at[tokens], sems.at[n, i])
                copy.start()
                copies.append(copy)
    for copy in copies:
        copy.wait()


def finish(k, v, gk_local, gv_local, arriving, last):
    return call(
        last_kernel,
        [VMEM, VMEM, VMEM, ANY, VMEM, ANY],
        [ANY] * 2,
        [struct((1024, 512), BF16)] * 2,
        scratch=[pltpu.VMEM((1024, 512), BF16)] * 3
        + [pltpu.VMEM((512, 128), F32)]
        + [pltpu.SemaphoreType.DMA((4,)), pltpu.SemaphoreType.DMA((2, 4)), pltpu.SemaphoreType.DMA],
        flops=2 * 2 * 1024 * 512 * 128,
        nbytes=8 << 20,
        vmem=LARGE,
    )(k, v, gk_local, gv_local, arriving, last)


def running(pieces, after, reverse):
    def kernel(pieces_ref, after_ref, out_ref):
        run = jnp.zeros(pieces_ref.shape[1:], F32)
        order = range(CTX - 1, -1, -1) if reverse else range(CTX)
        for i in order:
            out_ref[i] = run
            run = run + pieces_ref[i]

    return call(kernel, [VMEM, ANY], VMEM, struct(pieces.shape, F32), flops=1 << 17, nbytes=1 << 19, vmem=LARGE)(
        pieces, after
    )


def exchange(value):
    return lax.all_to_all(value, "ctx", 0, 0, tiled=True)


def split(total):
    return exchange(total.reshape(CTX, 512 // CTX, 128))


def merge(sums):
    return exchange(sums).reshape(512, 128)


def on_device(queries, keys, values, gain, grad_normed):
    gain = gain.reshape(1, 512)
    total = moments(keys, values)
    pieces = split(total)
    local, early, late, flip, first = local_attention(queries, keys, values)
    incoming = merge(running(pieces, local, False))
    att, stats = attend(queries, local, grad_normed, gain, incoming, first)
    stats = lax.all_to_all(stats, "head", 0, 0, tiled=True)
    normed, ga, cototal, last = norm(att, grad_normed, flip, gain, stats)
    pieces = split(cototal)
    gk_local, gv_local = back(queries, values, ga, early, late)
    arriving = merge(running(pieces, gv_local, True))
    gq = query_grad(keys, values, ga, incoming, first)
    gk, gv = finish(keys, values, gk_local, gv_local, arriving, last)
    return normed, gq, gk, gv


def solution(mesh):
    spec = P("ctx", "head")
    return jax.shard_map(
        on_device,
        mesh=mesh,
        in_specs=(spec, spec, spec, P("head"), spec),
        out_specs=(spec,) * 4,
        check_vma=False,
    )
```
